32 devices in a mesh: dp: 4 (over y, x), fsdp: 4 (over z), crop: 2 (over core).
Axes of the slice: x: 2, y: 2, z: 4, core: 2. Of those that a mesh axis runs over, the one named last changes fastest.
Arguments:
- grad_parts: float32 [8, 848, 1536], P(('dp', 'crop'), None, 'fsdp'), may hold values from -1.5 to 1.5
- student: float32 [848, 1536], P(('dp', 'crop'), 'fsdp'), may hold values from -2 to 2
- teacher: float32 [848, 1536], P(('dp', 'crop'), 'fsdp'), may hold values from -2 to 2
- moment1: float32 [848, 1536], P(('dp', 'crop'), 'fsdp'), may hold values from -0.6 to 0.6
- moment2: float32 [848, 1536], P(('dp', 'crop'), 'fsdp'), may hold values from 0.001 to 0.01
- step_count: int32 [1], replicated, may hold values from 1 to 1999
- pixels: bfloat16 [16, 2, 256, 588], P(('dp', 'fsdp'), 'crop'), may hold values from -5 to 5
- assign: int32 [16, 2], P(('dp', 'fsdp')), may hold values from 0 to 1, each once within a row
Outputs:
- student_new: float32 [848, 1536], P(('dp', 'crop'), 'fsdp')
- moment1_new: float32 [848, 1536], P(('dp', 'crop'), 'fsdp')
- moment2_new: float32 [848, 1536], P(('dp', 'crop'), 'fsdp')
- teacher_new: float32 [848, 1536], P(('dp', 'crop'), 'fsdp')
- student_step: float32 [848, 1536], P(('dp', 'crop'), 'fsdp')
- teacher_tokens: float32 [16, 2, 257, 1536], P(('dp', 'fsdp'))
The draws below stay inside these ranges and needn't reach their ends.
Inputs may be any that keep to these rules, and one draw needn't show every extreme that they name: `assign`: each row holds 0 and 1 once.
All inputs are finite; a program needn't handle non-finite values.
Results may differ from the reference program's by a relative error of at most 0.0003.
Values may be sent and summed in bfloat16 or wider, within the bound.
A program may use at most 64 MiB of HBM per device.

```python
import math
import jax
import jax.numpy as jnp
from jax import lax

D = 1536
GLOBALS = 2
PIX = 588
PATCHES = 256
ROWS = 848
REPLICAS = 8
IMAGES = 16


def table_rows(key):
    base = jax.random.normal(key, (ROWS, D), jnp.float32)
    base = jnp.clip(base, -4.0, 4.0)
    row_index = jnp.arange(ROWS)
    scale = jnp.where(row_index < PIX, 0.05 * PIX ** (-0.5), jnp.where(row_index < PIX + PATCHES, 0.025, jnp.where(row_index == PIX + PATCHES, 0.05, jnp.where(row_index == PIX + PATCHES + 1, 0.01, 0.2))))
    offset = jnp.where(row_index == PIX + PATCHES + 2, 1.0, 0.0)
    return base * scale[:, None] + offset[:, None]


def draw_student(key, part):
    return table_rows(jax.random.fold_in(key, 11))


def draw_teacher(key, part):
    return table_rows(jax.random.fold_in(key, 23))


def raised(entries, stream_key, source, target, shards_of, factor):
    def block_of(axis_at):
        return (jnp.arange(entries.shape[axis_at]) // (entries.shape[axis_at] // shards_of)).reshape((-1,) + (1,) * (entries.ndim - 1 - axis_at))

    first = jax.random.permutation(stream_key, shards_of)[block_of(target)]
    far = (block_of(target) + shards_of // 2) % shards_of
    return jnp.where((block_of(source) == first) | (block_of(source) == far), factor * entries, entries)


def level_of(stream_key, shape, pieces, least, top_value):
    level = 1.0
    for dim, parts in pieces:
        steps = jax.random.uniform(jax.random.fold_in(jax.random.fold_in(stream_key, 6), dim), (parts,), jnp.float32, least / len(pieces), top_value / len(pieces))
        level = level * jnp.repeat(jnp.exp(steps), shape[dim] // parts).reshape((-1,) + (1,) * (len(shape) - 1 - dim))
    return level


def bell_draw(stream_key, dims, deviation, limit, shards=(), kind=jnp.bfloat16):
    result = deviation * jax.random.normal(stream_key, dims, jnp.float32)
    if shards:
        result = result * level_of(stream_key, dims, shards, -0.22, 0.18)
    return jnp.clip(result, -limit, limit).astype(kind)


def bell_draw_with(own_key, dims, scale, limit, shards, heavy, held_as=jnp.bfloat16):
    drawn = scale * jax.random.normal(own_key, dims, jnp.float32)
    if shards:
        drawn = drawn * level_of(own_key, dims, shards, -0.22, 0.18)
    return jnp.clip(raised(drawn, jax.random.fold_in(own_key, 3), *heavy), -limit, limit).astype(held_as)


def setup_inputs(seed: int = 0) -> dict:
    splits = jax.random.split(jax.random.key(seed), 9)
    grad_parts = bell_draw_with(splits[0], (REPLICAS, ROWS, D), 0.25, 1.5, ((0, 8), (2, 4)), (0, 1, 8, 2.0), jnp.float32)
    student = draw_student(jax.random.fold_in(splits[8], 71), 0)
    teacher = draw_teacher(jax.random.fold_in(splits[8], 71), 0)
    moment1 = bell_draw(splits[3], (ROWS, D), 0.1, 0.6, ((0, 8), (1, 4)), jnp.float32)
    moment2 = jnp.clip(jnp.exp(math.log(0.01) - 2.30258502 * jax.random.uniform(splits[4], (ROWS, D), jnp.float32) ** level_of(splits[4], (ROWS, D), ((0, 8), (1, 4)), -0.2, 0.2)), 0.001, 0.01)
    step_count = jax.random.randint(splits[5], (1,), 1, 2000).astype(jnp.int32)
    pixels = bell_draw(splits[6], (IMAGES, GLOBALS, PATCHES, PIX), 1.0, 5.0, ((0, 16), (1, 2)))
    assign = jax.vmap(lambda own: jax.random.permutation(own, 2))(jax.random.split(splits[7], IMAGES)).reshape((IMAGES, GLOBALS)).astype(jnp.int32)
    return {"grad_parts": grad_parts, "student": student, "teacher": teacher, "moment1": moment1, "moment2": moment2, "step_count": step_count, "pixels": pixels, "assign": assign}


beta_one = 0.9
beta_two = 0.999
adam_epsilon = 1e-08
learn_rate = 0.001
weight_decay = 0.04
momentum_base = 0.992
plan_length = 625000.0
norm_epsilon = 1e-06

def optimize(gradient, student, teacher, moment1, moment2, step_count):
    step_value = step_count[0].astype(jnp.float32)
    first_moment = beta_one * moment1 + (1.0 - beta_one) * gradient
    second_moment = beta_two * moment2 + (1.0 - beta_two) * gradient * gradient
    first_fix = 1.0 - jnp.power(jnp.float32(beta_one), step_value)
    second_fix = 1.0 - jnp.power(jnp.float32(beta_two), step_value)
    update = first_moment / first_fix / (jnp.sqrt(second_moment / second_fix) + adam_epsilon) + weight_decay * student
    student_new = student - learn_rate * update
    momentum = 1.0 - (1.0 - momentum_base) * (jnp.cos(math.pi * step_value / plan_length) + 1.0) / 2.0
    teacher_new = momentum * teacher + (1.0 - momentum) * student_new
    return (student_new, first_moment, second_moment, teacher_new, update)

def embed(patches, table):
    count = patches.shape[0]
    pix_size = patches.shape[2]
    patch_count = patches.shape[1]
    width = table.shape[1]
    weight = table[:pix_size]
    position = table[pix_size:pix_size + patch_count]
    extras = table[pix_size + patch_count:]
    flat_patches = patches.reshape(count * patch_count, pix_size).astype(jnp.float32)
    projected = jnp.dot(flat_patches, weight, precision=lax.Precision.HIGHEST, preferred_element_type=jnp.float32)
    projected = projected.reshape(count, patch_count, width) + extras[1] + position
    class_row = jnp.broadcast_to(extras[0], (count, 1, width))
    tokens = jnp.concatenate([class_row, projected], axis=1)
    average = lax.optimization_barrier(jnp.mean(tokens, axis=-1, keepdims=True))
    centered = tokens - average
    variance = lax.optimization_barrier(jnp.mean(centered * centered, axis=-1, keepdims=True))
    return centered * lax.rsqrt(variance + norm_epsilon) * extras[2] + extras[3]

def reference(grad_parts, student, teacher, moment1, moment2, step_count, pixels, assign):
    gradient = lax.optimization_barrier(jnp.sum(grad_parts, axis=0))
    student_new, first_moment, second_moment, teacher_new, update = optimize(gradient, student, teacher, moment1, moment2, step_count)

    def one_image(items):
        crops, order = items
        both = embed(crops, teacher_new)
        return jnp.where((order == 0)[:, None, None], both[0][None], both[1][None])
    teacher_tokens = lax.map(one_image, (pixels, assign))
    return (student_new, first_moment, second_moment, teacher_new, update, teacher_tokens)
```

```python
import functools
import math

import jax
import jax.numpy as jnp
from jax import lax
from jax.experimental import pallas as pl
from jax.experimental.pallas import tpu as pltpu
from jax.sharding import PartitionSpec as P

beta_one = 0.9
beta_two = 0.999
adam_epsilon = 1e-08
learn_rate = 0.001
weight_decay = 0.04
momentum_base = 0.992
plan_length = 625000.0
norm_epsilon = 1e-06


def optimize(gradient, student, teacher, moment1, moment2, step_count):
    step_value = step_count[0].astype(jnp.float32)
    first_moment = beta_one * moment1 + (1.0 - beta_one) * gradient
    second_moment = beta_two * moment2 + (1.0 - beta_two) * gradient * gradient
    first_fix = 1.0 - jnp.power(jnp.float32(beta_one), step_value)
    second_fix = 1.0 - jnp.power(jnp.float32(beta_two), step_value)
    update = (
        first_moment / first_fix / (jnp.sqrt(second_moment / second_fix) + adam_epsilon)
        + weight_decay * student
    )
    student_new = student - learn_rate * update
    momentum = (
        1.0 - (1.0 - momentum_base) * (jnp.cos(math.pi * step_value / plan_length) + 1.0) / 2.0
    )
    teacher_new = momentum * teacher + (1.0 - momentum) * student_new
    return (student_new, first_moment, second_moment, teacher_new, update)


def embed(patches, table):
    count = patches.shape[0]
    pix_size = patches.shape[2]
    patch_count = patches.shape[1]
    width = table.shape[1]
    weight = table[:pix_size]
    position = table[pix_size : pix_size + patch_count]
    extras = table[pix_size + patch_count :]
    flat_patches = patches.reshape(count * patch_count, pix_size).astype(jnp.float32)
    projected = jnp.dot(
        flat_patches, weight, precision=lax.Precision.HIGHEST, preferred_element_type=jnp.float32
    )
    projected = projected.reshape(count, patch_count, width) + extras[1] + position
    class_row = jnp.broadcast_to(extras[0], (count, 1, width))
    tokens = jnp.concatenate([class_row, projected], axis=1)
    average = jnp.mean(tokens, axis=-1, keepdims=True)
    centered = tokens - average
    variance = jnp.mean(centered * centered, axis=-1, keepdims=True)
    return centered * lax.rsqrt(variance + norm_epsilon) * extras[2] + extras[3]


LEVELS = 32767.0
CODES = 256.0
MESH = pl.DeviceIdType.MESH


def padded_rows(rows):
    return -(-(rows + 1) // 16) * 16


def lanes_of(count):
    return -(-count // 128) * 128


def windows_fit(rows, count):
    size = padded_rows(rows)
    return all(j * rows % 8 + rows <= size and j * rows // 8 * 8 + size <= rows * count for j in range(count))


def turned(count, width, offset):
    row = lax.broadcasted_iota(jnp.int32, (count, width), 0) - offset
    return jnp.where(row < 0, row + count, row)


def encode(value, rows, offset):
    count, width = value.shape
    row_index = turned(count, width, offset)
    value = jnp.where(row_index < rows, value, 0.0)
    top = jnp.maximum(jnp.max(jnp.abs(value), axis=1, keepdims=True), 1e-30)
    code = jnp.ceil(jnp.log2(top) * CODES + 0.01)
    scaled = value * (jnp.exp2(code * (-1.0 / CODES)) * LEVELS)
    lanes = lanes_of(count)
    lane = lax.broadcasted_iota(jnp.int32, (count, lanes), 1)
    near = jnp.where(row_index[:, :lanes] == lane, code, 0.0)
    code_row = jnp.sum(near, axis=0, keepdims=True)
    if width > lanes:
        rest = jnp.zeros((1, width - lanes), jnp.float32)
        code_row = jnp.concatenate([code_row, rest], axis=1)
    out = jnp.where(row_index == rows, jnp.broadcast_to(code_row, (count, width)), scaled)
    out = jnp.clip(jnp.round(out), -LEVELS, LEVELS)
    return out.astype(jnp.int32).astype(jnp.int16)


def decode(block, rows, offset):
    count, width = block.shape
    value = block.astype(jnp.int32).astype(jnp.float32)
    lanes = lanes_of(count)
    lane = lax.broadcasted_iota(jnp.int32, (count, lanes), 1)
    row_index = turned(count, lanes, offset)
    if isinstance(offset, int):
        code_row = value[rows : rows + 1, :lanes]
    else:
        code_row = jnp.sum(jnp.where(row_index == rows, value[:, :lanes], 0.0), axis=0, keepdims=True)
    near = jnp.where(row_index == lane, code_row, 0.0)
    code = jnp.sum(near, axis=1, keepdims=True)
    return value * (jnp.exp2(code * (1.0 / CODES)) * (1.0 / LEVELS))


OWN = 4
ORDER = (
    (1, 0), (2, 0), (3, 0), (0, 1), (0, 2), (1, 2), (2, 1), (3, 1), (3, 2), (0, 3), (2, 2),
    (1, 1), (1, 3), (2, 3), (3, 3),
)
DIRECT = (0, 3)
LAG = 2


def schedule(step_ref):
    step_value = jnp.full((8, 128), step_ref[0], jnp.int32).astype(jnp.float32)
    first_fix = 1.0 - jnp.power(jnp.full((8, 128), beta_one, jnp.float32), step_value)
    second_fix = 1.0 - jnp.power(jnp.full((8, 128), beta_two, jnp.float32), step_value)
    momentum = (
        1.0 - (1.0 - momentum_base) * (jnp.cos(math.pi * step_value / plan_length) + 1.0) / 2.0
    )
    return first_fix[0:1, 0:1], second_fix[0:1, 0:1], momentum[0:1, 0:1]


def step_of(gradient, student, teacher, moment1, moment2, step_ref):
    first_fix, second_fix, momentum = schedule(step_ref)
    first_moment = beta_one * moment1 + (1.0 - beta_one) * gradient
    second_moment = beta_two * moment2 + (1.0 - beta_two) * gradient * gradient
    update = (
        first_moment / first_fix / (jnp.sqrt(second_moment / second_fix) + adam_epsilon)
        + weight_decay * student
    )
    student_new = student - learn_rate * update
    teacher_new = momentum * teacher + (1.0 - momentum) * student_new
    return student_new, first_moment, second_moment, teacher_new, update


def hops_of(q, who):
    if who == 0:
        return ((OWN + 1, OWN + 2, OWN + 3) if q == 0 else ()) + ((3,) if q in DIRECT else ()) + (1, 2)
    if q in DIRECT or who == 3:
        return ()
    return (3 - who,) if (q % 2 == 0) == (who == 1) else ()


def refresh_kernel(
    sizes, grad_ref, pixel_ref, student_ref, teacher_ref, moment1_ref, moment2_ref, pick_ref, step_ref,
    state_ref, x_ref, extra_ref, same_ref,
    table_ref, weight_ref, left_ref, pixels_ref, mine_ref, other_ref, half_ref, pre_ref, out_ref, in_ref,
    space_ref, held_ref, pick_now,
    load_sem, half_sem, pair_sem, out_sem, in_sem, pix_sem, go_sem, come_sem, share_sem, gone_sem,
):
    DP, F, C = sizes
    rows, size = student_ref.shape[0], table_ref.shape[3]
    d, f, c = lax.axis_index("dp"), lax.axis_index("fsdp"), lax.axis_index("crop")
    partner = lax.rem(c + 1, C)

    barrier = pltpu.get_barrier_semaphore()
    pl.semaphore_signal(barrier, inc=1, device_id={"crop": partner}, device_id_type=MESH)
    for r in range(1, DP):
        pl.semaphore_signal(barrier, inc=1, device_id={"dp": lax.rem(d + r, DP)}, device_id_type=MESH)
    for r in range(1, F):
        pl.semaphore_signal(barrier, inc=1, device_id={"fsdp": lax.rem(f + r, F)}, device_id_type=MESH)

    order = [DP - r for r in range(1, DP)] + [0]

    def window(at, core):
        start = (at * C + core) * rows // 8 * 8
        return grad_ref.at[0, pl.ds(pl.multiple_of(start, 8), size)]

    halves = []
    for r in order:
        copy = pltpu.make_async_copy(window(lax.rem(d + r, DP), c), half_ref.at[r], half_sem.at[r])
        copy.start()
        halves.append(copy)
    loads = []
    for source, target in (
        (pick_ref, pick_now), (pixel_ref, mine_ref), (student_ref, held_ref.at[0]),
        (teacher_ref, held_ref.at[1]), (moment1_ref, held_ref.at[2]), (moment2_ref, held_ref.at[3]),
    ):
        copy = pltpu.make_async_copy(source, target, load_sem.at[len(loads)])
        copy.start()
        loads.append(copy)

    pl.semaphore_wait(barrier, DP - 1 + 1 + F - 1)
    sends = []
    for r in order:
        copy = pltpu.make_async_remote_copy(
            src_ref=window(lax.rem(d + r, DP), partner), dst_ref=pre_ref.at[r],
            send_sem=pair_sem.at[0, r], recv_sem=pair_sem.at[1, r],
            device_id={"crop": partner}, device_id_type=MESH,
        )
        copy.start()
        sends.append(copy)
    blocks = []
    total = None
    offset = (d * C + c) * rows % 8
    for number, r in enumerate(order):
        at = lax.rem(d + r, DP)
        halves[number].wait()
        sends[number].wait_recv()
        chip = half_ref[r] + pre_ref[r]
        if r == 0:
            total = chip
            break
        out_ref[r] = encode(chip, rows, (at * C + c) * rows % 8)
        copy = pltpu.make_async_remote_copy(
            src_ref=out_ref.at[r], dst_ref=in_ref.at[r],
            send_sem=out_sem.at[r], recv_sem=in_sem.at[r],
            device_id={"dp": at}, device_id_type=MESH,
        )
        copy.start()
        blocks.append(copy)
    pixel_copy = pltpu.make_async_remote_copy(
        src_ref=pixel_ref, dst_ref=other_ref, send_sem=pix_sem.at[0], recv_sem=pix_sem.at[1],
        device_id={"crop": partner}, device_id_type=MESH,
    )
    pixel_copy.start()
    for copy in loads:
        copy.wait()

    slot = weight_ref.shape[4]
    pix_size, patch_count = pixel_ref.shape
    base = pix_size + patch_count

    def prepare(k, source_ref):
        pixels_ref[0:pix_size] = source_ref[...].astype(jnp.float32)
        pixels_ref[pix_size:] = jnp.zeros((pixels_ref.shape[0] - pix_size, patch_count), jnp.float32)
        for j in range(DP * C):
            lane = lax.broadcasted_iota(jnp.int32, (patch_count, slot), 1)
            patch = lax.broadcasted_iota(jnp.int32, (patch_count, slot), 0)
            at = lane + j * rows
            inside = lane < rows
            one = inside & ((at == base + 1) | ((at < base) & (at - pix_size == patch)))
            block = jnp.where(one, 1.0, 0.0)
            if j * rows < pix_size:
                block = block + jnp.where(inside, pixels_ref[j * rows : j * rows + slot].T, 0.0)
            part = slice(j % C * slot, (j % C + 1) * slot)
            left_ref[k, j // C, :, part] = block.astype(jnp.bfloat16)

    blank = jnp.zeros((2, F, DP, C, slot - size, weight_ref.shape[5]), jnp.bfloat16)
    weight_ref[:, :, :, :, size:] = blank
    prepare(0, mine_ref)
    for k in range(C):
        same_ref[k] = jnp.where(jnp.full(same_ref.shape[1:], pick_now[0, k], jnp.int32) == c, 1.0, 0.0)
    for number, copy in enumerate(blocks):
        copy.wait_recv()
        total = total + decode(in_ref[order[number]], rows, offset)
    gradient = pltpu.roll(total, lax.rem(size - offset, size), 0)[0:rows]
    fresh = step_of(gradient, held_ref[0], held_ref[1], held_ref[2], held_ref[3], step_ref)
    space_ref[rows:] = jnp.zeros((size - rows, space_ref.shape[1]), jnp.float32)
    space_ref[0:rows] = fresh[3]
    table_ref[0, 0, 0] = encode(space_ref[...], rows, 0)

    mid = (f == 1) | (f == 2)
    away = jnp.where(f < 2, 1, -1)
    planes = (
        f,
        jnp.where(mid, f - away, f + away),
        jnp.where(mid, f + away, f + 2 * away),
        jnp.where(mid, f + 2 * away, f + 3 * away),
    )
    slots = (0, 1, jnp.where(mid, 2, 3), jnp.where(mid, 2, 3))
    row, column = d // 2, lax.rem(d, 2)
    chips = (
        d,
        row * 2 + 1 - column,
        (1 - row) * 2 + column,
        (1 - row) * 2 + 1 - column,
    )

    def copy_to(q, who, hop):
        if hop < OWN:
            to, there = {"dp": chips[hop]}, (q, who ^ hop)
        else:
            to, there = {"fsdp": planes[hop - OWN]}, (slots[hop - OWN], who)
        return pltpu.make_async_remote_copy(
            src_ref=table_ref.at[0, q, who], dst_ref=table_ref.at[(0, *there)],
            send_sem=go_sem.at[q, who, hop], recv_sem=come_sem.at[there],
            device_id=to, device_id_type=MESH,
        )

    def pass_on(q, who):
        for hop in hops_of(q, who):
            copy_to(q, who, hop).start()
        pltpu.make_async_remote_copy(
            src_ref=table_ref.at[0, q, who], dst_ref=table_ref.at[1, q, who],
            send_sem=gone_sem.at[0], recv_sem=share_sem.at[q, who],
            device_id={"crop": partner}, device_id_type=MESH,
        ).start()

    def arrive(core, q, who):
        block = table_ref.at[core, q, who]
        sem = share_sem.at[q, who] if core else come_sem.at[q, who]
        pltpu.make_async_copy(block, block, sem).wait()

    def unpack(core, q, who):
        value = decode(table_ref[core, q, who], rows, 0)
        high = value.astype(jnp.bfloat16)
        place = (c, partner)[core]
        weight_ref[0, q, who, place, 0:size] = high
        weight_ref[1, q, who, place, 0:size] = (value - high.astype(jnp.float32)).astype(jnp.bfloat16)

    def multiply(q, who, first):
        for k in range(C):
            left = left_ref[k, chips[who]]
            part = None
            for level in range(2):
                right = weight_ref[level, q, who].reshape(C * slot, weight_ref.shape[5])
                now = jnp.dot(left, right, preferred_element_type=jnp.float32)
                part = now if part is None else part + now
            x_ref[q, k] = part if first else x_ref[q, k] + part

    pass_on(0, 0)
    for number in range(5):
        state_ref[number] = fresh[number]
    pixel_copy.wait()
    prepare(1, other_ref)
    started = []

    def finish(q, who):
        arrive(1, q, who)
        unpack(1, q, who)
        multiply(q, who, q not in started)
        started.append(q)

    unpack(0, 0, 0)
    ready = [(0, 0)]
    for q, who in ORDER:
        arrive(0, q, who)
        pass_on(q, who)
        unpack(0, q, who)
        ready.append((q, who))
        if len(ready) > LAG:
            finish(*ready.pop(0))
    for q, who in ready:
        finish(q, who)
    last = rows - (rows * DP * C - base)
    begin = last // 16 * 16
    for q in range(F):
        for who in range(DP):
            @pl.when(chips[who] == DP - 1)
            def _():
                extra_ref[q] = (
                    weight_ref[0, q, who, C - 1, begin:size].astype(jnp.float32)
                    + weight_ref[1, q, who, C - 1, begin:size].astype(jnp.float32)
                )
    pltpu.make_async_copy(table_ref.at[0], table_ref.at[0], gone_sem.at[0]).wait()
    for copy in blocks + sends:
        copy.wait_send()
    for q, who in ((0, 0),) + ORDER:
        for hop in hops_of(q, who):
            copy_to(q, who, hop).wait_send()


def tokens_kernel(
    sizes, state_ref, x_ref, extra_ref, same_ref,
    student_out, moment1_out, moment2_out, teacher_out, update_out, tokens_ref,
    stage_ref, sems, state_sems,
):
    DP, F, C = sizes
    f = lax.axis_index("fsdp")
    rows = state_ref.shape[1]
    patch_count = x_ref.shape[2]
    copies = []
    for number, target in enumerate((student_out, moment1_out, moment2_out, teacher_out, update_out)):
        copy = pltpu.make_async_copy(state_ref.at[number], target, state_sems.at[number])
        copy.start()
        copies.append(copy)
    mid = (f == 1) | (f == 2)
    away = jnp.where(f < 2, 1, -1)

    def place(i):
        inner = jnp.where(i == f, 0, jnp.where(i == f - away, 1, jnp.where(i == f + away, 2, 3)))
        return jnp.where(mid, inner, jnp.abs(i - f))

    places = [place(i) for i in range(F)]
    offset = (rows - 4) % 16

    def extra(n):
        return jnp.concatenate([extra_ref[at, offset + n : offset + n + 1] for at in places], axis=1)

    gain, shift = extra(2), extra(3)

    def normed(x):
        average = jnp.mean(x, axis=-1, keepdims=True)
        centered = x - average
        variance = jnp.mean(centered * centered, axis=-1, keepdims=True)
        return centered * lax.rsqrt(variance + norm_epsilon) * gain + shift

    class_row = normed(extra(0))
    for k in range(C):
        stage_ref[0:1, k] = class_row
    step = 32
    begun = 0
    picks = [jnp.broadcast_to(same_ref[k, 0:1, 0:1], (step, stage_ref.shape[2])) > 0.5 for k in range(C)]
    for number, start in enumerate(range(0, patch_count, step)):
        mine, other = (
            normed(jnp.concatenate([x_ref[at, k, start : start + step] for at in places], axis=1))
            for k in range(C)
        )
        for k in range(C):
            stage_ref[start + 1 : start + 1 + step, k] = jnp.where(picks[k], mine, other)
        end = start + 1 + step
        copy = pltpu.make_async_copy(
            stage_ref.at[begun:end], tokens_ref.at[begun:end], sems.at[number]
        )
        copy.start()
        copies.append(copy)
        begun = end
    for copy in copies:
        copy.wait()


def kernels(grad_parts, student, teacher, moment1, moment2, step_count, pixels, assign, sizes):
    DP, F, C = sizes
    rows, columns = student.shape
    spare = padded_rows(rows)
    slot = lanes_of(spare)
    own = pixels[0, 0].T
    pix_size, patch_count = own.shape
    here = pl.BlockSpec(memory_space=pltpu.VMEM)
    anywhere = pl.BlockSpec(memory_space=pl.ANY)
    scalars = pl.BlockSpec(memory_space=pltpu.SMEM)
    count = DP * C
    slab = spare - (rows - 4) // 16 * 16
    inputs = [
        pltpu.with_memory_space_constraint(value, pltpu.HBM)
        for value in (grad_parts, own, student, teacher, moment1, moment2, assign)
    ]
    shared = pl.pallas_call(
        functools.partial(refresh_kernel, sizes),
        out_shape=(
            pltpu.VMEM((5, rows, columns), jnp.float32),
            pltpu.VMEM((F, C, patch_count, columns), jnp.float32),
            pltpu.VMEM((F, slab, columns), jnp.float32),
            pltpu.VMEM((C, 8, 128), jnp.float32),
        ),
        in_specs=[anywhere] * 7 + [scalars],
        out_specs=(here,) * 4,
        scratch_shapes=[
            pltpu.VMEM((C, F, DP, spare, columns), jnp.int16),
            pltpu.VMEM((2, F, DP, C, slot, columns), jnp.bfloat16),
            pltpu.VMEM((C, DP, patch_count, C * slot), jnp.bfloat16),
            pltpu.VMEM((rows * (count - 1) + slot, patch_count), jnp.float32),
            pltpu.VMEM(own.shape, own.dtype),
            pltpu.VMEM(own.shape, own.dtype),
            pltpu.VMEM((DP, spare, columns), jnp.float32),
            pltpu.VMEM((DP, spare, columns), jnp.float32),
            pltpu.VMEM((DP, spare, columns), jnp.int16),
            pltpu.VMEM((DP, spare, columns), jnp.int16),
            pltpu.VMEM((spare, columns), jnp.float32),
            pltpu.VMEM((4, rows, columns), jnp.float32),
            pltpu.SMEM((1, C), jnp.int32),
            pltpu.SemaphoreType.DMA((6,)),
            pltpu.SemaphoreType.DMA((DP,)),
            pltpu.SemaphoreType.DMA((2, DP)),
            pltpu.SemaphoreType.DMA((DP,)),
            pltpu.SemaphoreType.DMA((DP,)),
            pltpu.SemaphoreType.DMA((2,)),
            pltpu.SemaphoreType.DMA((F, DP, OWN + F)),
            pltpu.SemaphoreType.DMA((F, DP)),
            pltpu.SemaphoreType.DMA((F, DP)),
            pltpu.SemaphoreType.DMA((1,)),
        ],
        compiler_params=pltpu.CompilerParams(
            collective_id=0, has_side_effects=True, vmem_limit_bytes=40 * 1024 * 1024
        ),
    )(*inputs, step_count)
    *results, tokens = pl.pallas_call(
        functools.partial(tokens_kernel, sizes),
        out_shape=(jax.ShapeDtypeStruct((rows, columns), jnp.float32),) * 5
        + (jax.ShapeDtypeStruct((patch_count + 1, C, columns * F), jnp.float32),),
        in_specs=[here] * 4,
        out_specs=(anywhere,) * 6,
        scratch_shapes=[
            pltpu.VMEM((patch_count + 1, C, columns * F), jnp.float32),
            pltpu.SemaphoreType.DMA((patch_count // 32,)),
            pltpu.SemaphoreType.DMA((5,)),
        ],
        compiler_params=pltpu.CompilerParams(vmem_limit_bytes=40 * 1024 * 1024),
    )(*(pltpu.with_memory_space_constraint(value, pltpu.VMEM) for value in shared))
    return (*results, tokens.transpose(1, 0, 2)[None])


def shards(grad_parts, student, teacher, moment1, moment2, step_count, pixels, assign):
    gradient = lax.psum_scatter(grad_parts[0], ("dp", "crop"), scatter_dimension=0, tiled=True)
    student_new, first_moment, second_moment, teacher_new, update = optimize(
        gradient, student, teacher, moment1, moment2, step_count
    )
    column_block = lax.all_gather(teacher_new, "fsdp", axis=1, tiled=True)
    gathered = lax.all_gather(column_block, ("dp", "crop"), axis=0, tiled=True)
    own_tokens = embed(pixels[:, 0], gathered)
    both = lax.all_gather(own_tokens[:, None], "crop", axis=1, tiled=True)
    teacher_tokens = jnp.where((assign == 0)[:, :, None, None], both[:, 0:1], both[:, 1:2])
    return (student_new, first_moment, second_moment, teacher_new, update, teacher_tokens)


def solution(mesh):
    placed = (
        P(("dp", "crop"), None, "fsdp"),
        P(("dp", "crop"), "fsdp"),
        P(("dp", "crop"), "fsdp"),
        P(("dp", "crop"), "fsdp"),
        P(("dp", "crop"), "fsdp"),
        P(),
        P(("dp", "fsdp"), "crop", None, None),
        P(("dp", "fsdp"), None),
    )
    sizes = (mesh.shape["dp"], mesh.shape["fsdp"], mesh.shape["crop"])

    def run(*args):
        grad_parts, student, pixels = args[0], args[1], args[6]
        fits = (
            student.shape[1] % 128 == 0
            and padded_rows(student.shape[0]) <= student.shape[1]
            and pixels.shape[:2] == (1, 1)
            and grad_parts.shape[0] == 1
            and sizes[0] == 4
            and sizes[1] == 4
            and pixels.shape[2] % 32 == 0
            and windows_fit(student.shape[0], sizes[0] * sizes[2])
            and sizes[2] == 2
        )
        return kernels(*args, sizes) if fits else shards(*args)

    return jax.shard_map(
        run,
        mesh=mesh,
        in_specs=placed,
        out_specs=(
            P(("dp", "crop"), "fsdp"),
            P(("dp", "crop"), "fsdp"),
            P(("dp", "crop"), "fsdp"),
            P(("dp", "crop"), "fsdp"),
            P(("dp", "crop"), "fsdp"),
            P(("dp", "fsdp"), None, None, None),
        ),
        check_vma=False,
    )
```

```python
import functools
import math

import jax
import jax.numpy as jnp
from jax import lax
from jax.experimental import pallas as pl
from jax.experimental.pallas import tpu as pltpu
from jax.sharding import PartitionSpec as P

beta_one = 0.9
beta_two = 0.999
adam_epsilon = 1e-08
learn_rate = 0.001
weight_decay = 0.04
momentum_base = 0.992
plan_length = 625000.0
norm_epsilon = 1e-06


def optimize(gradient, student, teacher, moment1, moment2, step_count):
    step_value = step_count[0].astype(jnp.float32)
    first_moment = beta_one * moment1 + (1.0 - beta_one) * gradient
    second_moment = beta_two * moment2 + (1.0 - beta_two) * gradient * gradient
    first_fix = 1.0 - jnp.power(jnp.float32(beta_one), step_value)
    second_fix = 1.0 - jnp.power(jnp.float32(beta_two), step_value)
    update = (
        first_moment / first_fix / (jnp.sqrt(second_moment / second_fix) + adam_epsilon)
        + weight_decay * student
    )
    student_new = student - learn_rate * update
    momentum = (
        1.0 - (1.0 - momentum_base) * (jnp.cos(math.pi * step_value / plan_length) + 1.0) / 2.0
    )
    teacher_new = momentum * teacher + (1.0 - momentum) * student_new
    return (student_new, first_moment, second_moment, teacher_new, update)


def embed(patches, table):
    count = patches.shape[0]
    pix_size = patches.shape[2]
    patch_count = patches.shape[1]
    width = table.shape[1]
    weight = table[:pix_size]
    position = table[pix_size : pix_size + patch_count]
    extras = table[pix_size + patch_count :]
    flat_patches = patches.reshape(count * patch_count, pix_size).astype(jnp.float32)
    projected = jnp.dot(
        flat_patches, weight, precision=lax.Precision.HIGHEST, preferred_element_type=jnp.float32
    )
    projected = projected.reshape(count, patch_count, width) + extras[1] + position
    class_row = jnp.broadcast_to(extras[0], (count, 1, width))
    tokens = jnp.concatenate([class_row, projected], axis=1)
    average = jnp.mean(tokens, axis=-1, keepdims=True)
    centered = tokens - average
    variance = jnp.mean(centered * centered, axis=-1, keepdims=True)
    return centered * lax.rsqrt(variance + norm_epsilon) * extras[2] + extras[3]


LEVELS = 32767.0
CODES = 256.0
MESH = pl.DeviceIdType.MESH


def padded_rows(rows):
    return -(-(rows + 1) // 16) * 16


def lanes_of(count):
    return -(-count // 128) * 128


def windows_fit(rows, count):
    size = padded_rows(rows)
    return all(j * rows % 8 + rows <= size and j * rows // 8 * 8 + size <= rows * count for j in range(count))


def turned(count, width, offset):
    row = lax.broadcasted_iota(jnp.int32, (count, width), 0) - offset
    return jnp.where(row < 0, row + count, row)


def encode(value, rows, offset):
    count, width = value.shape
    row_index = turned(count, width, offset)
    value = jnp.where(row_index < rows, value, 0.0)
    top = jnp.maximum(jnp.max(jnp.abs(value), axis=1, keepdims=True), 1e-30)
    code = jnp.ceil(jnp.log2(top) * CODES + 0.01)
    scaled = value * (jnp.exp2(code * (-1.0 / CODES)) * LEVELS)
    lanes = lanes_of(count)
    lane = lax.broadcasted_iota(jnp.int32, (count, lanes), 1)
    near = jnp.where(row_index[:, :lanes] == lane, code, 0.0)
    code_row = jnp.sum(near, axis=0, keepdims=True)
    if width > lanes:
        rest = jnp.zeros((1, width - lanes), jnp.float32)
        code_row = jnp.concatenate([code_row, rest], axis=1)
    out = jnp.where(row_index == rows, jnp.broadcast_to(code_row, (count, width)), scaled)
    out = jnp.clip(jnp.round(out), -LEVELS, LEVELS)
    return out.astype(jnp.int32).astype(jnp.int16)


def decode(block, rows, offset):
    count, width = block.shape
    value = block.astype(jnp.int32).astype(jnp.float32)
    lanes = lanes_of(count)
    lane = lax.broadcasted_iota(jnp.int32, (count, lanes), 1)
    row_index = turned(count, lanes, offset)
    if isinstance(offset, int):
        code_row = value[rows : rows + 1, :lanes]
    else:
        code_row = jnp.sum(jnp.where(row_index == rows, value[:, :lanes], 0.0), axis=0, keepdims=True)
    near = jnp.where(row_index == lane, code_row, 0.0)
    code = jnp.sum(near, axis=1, keepdims=True)
    return value * (jnp.exp2(code * (1.0 / CODES)) * (1.0 / LEVELS))


OWN = 4
ORDER = (
    (1, 0), (0, 1), (0, 2), (2, 0), (3, 0), (0, 3), (1, 1), (1, 3), (1, 2), (2, 1), (2, 2),
    (3, 1), (3, 2), (2, 3), (3, 3),
)
GROUPS = ((0, 1, 2), (3,))
LAG = 2


def schedule(step_ref):
    step_value = jnp.full((8, 128), step_ref[0], jnp.int32).astype(jnp.float32)
    first_fix = 1.0 - jnp.power(jnp.full((8, 128), beta_one, jnp.float32), step_value)
    second_fix = 1.0 - jnp.power(jnp.full((8, 128), beta_two, jnp.float32), step_value)
    momentum = (
        1.0 - (1.0 - momentum_base) * (jnp.cos(math.pi * step_value / plan_length) + 1.0) / 2.0
    )
    return first_fix[0:1, 0:1], second_fix[0:1, 0:1], momentum[0:1, 0:1]


def step_of(gradient, student, teacher, moment1, moment2, step_ref):
    first_fix, second_fix, momentum = schedule(step_ref)
    first_moment = beta_one * moment1 + (1.0 - beta_one) * gradient
    second_moment = beta_two * moment2 + (1.0 - beta_two) * gradient * gradient
    update = (
        first_moment / first_fix / (jnp.sqrt(second_moment / second_fix) + adam_epsilon)
        + weight_decay * student
    )
    student_new = student - learn_rate * update
    teacher_new = momentum * teacher + (1.0 - momentum) * student_new
    return student_new, first_moment, second_moment, teacher_new, update


def hops_of(q, who):
    if who == 0:
        along = (OWN + 1, OWN + 3, OWN + 2) if q == 0 else ()
        return along + ((3,) if q in (0, 3) else ()) + (1, 2), ()
    if who == 3 and q == 0:
        return (OWN + 1,), (OWN + 2,)
    if who == 3 and q == 1:
        return (), (OWN + 2,)
    return (), ()


def refresh_kernel(
    sizes, grad_ref, pixel_ref, student_ref, teacher_ref, moment1_ref, moment2_ref, pick_ref, step_ref,
    state_ref, x_ref, extra_ref, same_ref,
    table_ref, weight_ref, left_ref, pixels_ref, mine_ref, other_ref, half_ref, pre_ref, out_ref, in_ref,
    space_ref, held_ref, pick_now,
    load_sem, half_sem, pair_sem, out_sem, in_sem, pix_sem, go_sem, come_sem, share_sem, gone_sem,
):
    DP, F, C = sizes
    rows, size = student_ref.shape[0], table_ref.shape[3]
    d, f, c = lax.axis_index("dp"), lax.axis_index("fsdp"), lax.axis_index("crop")
    partner = lax.rem(c + 1, C)

    barrier = pltpu.get_barrier_semaphore()
    pl.semaphore_signal(barrier, inc=1, device_id={"crop": partner}, device_id_type=MESH)
    for r in range(1, DP):
        pl.semaphore_signal(barrier, inc=1, device_id={"dp": lax.rem(d + r, DP)}, device_id_type=MESH)
    for r in range(1, F):
        pl.semaphore_signal(barrier, inc=1, device_id={"fsdp": lax.rem(f + r, F)}, device_id_type=MESH)

    order = [DP - r for r in range(1, DP)] + [0]

    def window(at, core):
        start = (at * C + core) * rows // 8 * 8
        return grad_ref.at[0, pl.ds(pl.multiple_of(start, 8), size)]

    halves = []
    for r in order:
        copy = pltpu.make_async_copy(window(lax.rem(d + r, DP), c), half_ref.at[r], half_sem.at[r])
        copy.start()
        halves.append(copy)
    loads = []
    for source, target in (
        (pick_ref, pick_now), (pixel_ref, mine_ref), (student_ref, held_ref.at[0]),
        (teacher_ref, held_ref.at[1]), (moment1_ref, held_ref.at[2]), (moment2_ref, held_ref.at[3]),
    ):
        copy = pltpu.make_async_copy(source, target, load_sem.at[len(loads)])
        copy.start()
        loads.append(copy)

    pl.semaphore_wait(barrier, DP - 1 + 1 + F - 1)
    sends = []
    for r in order:
        copy = pltpu.make_async_remote_copy(
            src_ref=window(lax.rem(d + r, DP), partner), dst_ref=pre_ref.at[r],
            send_sem=pair_sem.at[0, r], recv_sem=pair_sem.at[1, r],
            device_id={"crop": partner}, device_id_type=MESH,
        )
        copy.start()
        sends.append(copy)
    blocks = []
    total = None
    offset = (d * C + c) * rows % 8
    for number, r in enumerate(order):
        at = lax.rem(d + r, DP)
        halves[number].wait()
        sends[number].wait_recv()
        chip = half_ref[r] + pre_ref[r]
        if r == 0:
            total = chip
            break
        out_ref[r] = encode(chip, rows, (at * C + c) * rows % 8)
        copy = pltpu.make_async_remote_copy(
            src_ref=out_ref.at[r], dst_ref=in_ref.at[r],
            send_sem=out_sem.at[r], recv_sem=in_sem.at[r],
            device_id={"dp": at}, device_id_type=MESH,
        )
        copy.start()
        blocks.append(copy)
    pixel_copy = pltpu.make_async_remote_copy(
        src_ref=pixel_ref, dst_ref=other_ref, send_sem=pix_sem.at[0], recv_sem=pix_sem.at[1],
        device_id={"crop": partner}, device_id_type=MESH,
    )
    pixel_copy.start()
    for copy in loads:
        copy.wait()

    slot = weight_ref.shape[4]
    depth = 2 * C * slot
    row, column = d // 2, lax.rem(d, 2)
    pix_size, patch_count = pixel_ref.shape
    base = pix_size + patch_count

    def prepare(k, source_ref):
        pixels_ref[0:pix_size] = source_ref[...].astype(jnp.float32)
        pixels_ref[pix_size:] = jnp.zeros((pixels_ref.shape[0] - pix_size, patch_count), jnp.float32)
        for j in range(DP * C):
            lane = lax.broadcasted_iota(jnp.int32, (patch_count, slot), 1)
            patch = lax.broadcasted_iota(jnp.int32, (patch_count, slot), 0)
            at = lane + j * rows
            inside = lane < rows
            one = inside & ((at == base + 1) | ((at < base) & (at - pix_size == patch)))
            block = jnp.where(one, 1.0, 0.0)
            if j * rows < pix_size:
                block = block + jnp.where(inside, pixels_ref[j * rows : j * rows + slot].T, 0.0)
            near = lax.rem(j // C // 2 + row, 2) * 2 + lax.rem(j // C + column, 2)
            block = block.astype(jnp.bfloat16)
            for level in range(2):
                start = near * depth + (level * C + j % C) * slot
                left_ref[k, :, pl.ds(pl.multiple_of(start, 128), slot)] = block

    blank = jnp.zeros((F, DP, 2, C, slot - size, weight_ref.shape[5]), jnp.bfloat16)
    weight_ref[:, :, :, :, size:] = blank
    prepare(0, mine_ref)
    for k in range(C):
        same_ref[k] = jnp.where(jnp.full(same_ref.shape[1:], pick_now[0, k], jnp.int32) == c, 1.0, 0.0)
    for number, copy in enumerate(blocks):
        copy.wait_recv()
        total = total + decode(in_ref[order[number]], rows, offset)
    gradient = pltpu.roll(total, lax.rem(size - offset, size), 0)[0:rows]
    fresh = step_of(gradient, held_ref[0], held_ref[1], held_ref[2], held_ref[3], step_ref)
    space_ref[rows:] = jnp.zeros((size - rows, space_ref.shape[1]), jnp.float32)
    space_ref[0:rows] = fresh[3]
    table_ref[0, 0, 0] = encode(space_ref[...], rows, 0)

    mid = (f == 1) | (f == 2)
    away = jnp.where(f < 2, 1, -1)
    planes = (
        f,
        f + away,
        jnp.where(mid, f - away, f + 2 * away),
        jnp.where(mid, f + 2 * away, f + 3 * away),
    )
    slots = (0, jnp.where(mid, 1, 2), jnp.where(mid, 1, 3), jnp.where(mid, 2, 3))
    chips = (
        d,
        row * 2 + 1 - column,
        (1 - row) * 2 + column,
        (1 - row) * 2 + 1 - column,
    )

    def copy_to(q, who, hop):
        if hop < OWN:
            to, there = {"dp": chips[hop]}, (q, who ^ hop)
        else:
            to = {"fsdp": planes[hop - OWN]}
            there = (slots[hop - OWN] if q == 0 else 2, who)
        return pltpu.make_async_remote_copy(
            src_ref=table_ref.at[0, q, who], dst_ref=table_ref.at[(0, *there)],
            send_sem=go_sem.at[q, who, hop], recv_sem=come_sem.at[there],
            device_id=to, device_id_type=MESH,
        )

    def pass_on(q, who):
        always, inner = hops_of(q, who)
        for hop in always:
            copy_to(q, who, hop).start()
        for hop in inner:
            pl.when(mid)(copy_to(q, who, hop).start)
        pltpu.make_async_remote_copy(
            src_ref=table_ref.at[0, q, who], dst_ref=table_ref.at[1, q, who],
            send_sem=gone_sem.at[0], recv_sem=share_sem.at[q, who],
            device_id={"crop": partner}, device_id_type=MESH,
        ).start()

    def arrive(core, q, who):
        block = table_ref.at[core, q, who]
        sem = share_sem.at[q, who] if core else come_sem.at[q, who]
        pltpu.make_async_copy(block, block, sem).wait()

    def unpack(core, q, who):
        value = decode(table_ref[core, q, who], rows, 0)
        high = value.astype(jnp.bfloat16)
        place = (c, partner)[core]
        weight_ref[q, who, 0, place, 0:size] = high
        weight_ref[q, who, 1, place, 0:size] = (value - high.astype(jnp.float32)).astype(jnp.bfloat16)

    started = set()

    def multiply(q, group):
        first, last = group[0], group[-1] + 1
        right = weight_ref[q, first:last].reshape((last - first) * depth, weight_ref.shape[5])
        for k in range(C):
            left = left_ref[k, :, first * depth : last * depth]
            now = jnp.dot(left, right, preferred_element_type=jnp.float32)
            x_ref[q, k] = x_ref[q, k] + now if q in started else now
        started.add(q)

    pass_on(0, 0)
    for number in range(5):
        state_ref[number] = fresh[number]
    pixel_copy.wait()
    prepare(1, other_ref)
    seen = set()

    def finish(q, who):
        arrive(1, q, who)
        unpack(1, q, who)
        seen.add((q, who))
        for group in GROUPS:
            if who in group and all((q, other) in seen for other in group):
                multiply(q, group)

    unpack(0, 0, 0)
    ready = [(0, 0)]
    for q, who in ORDER:
        arrive(0, q, who)
        pass_on(q, who)
        unpack(0, q, who)
        ready.append((q, who))
        if len(ready) > LAG:
            finish(*ready.pop(0))
    for q, who in ready:
        finish(q, who)
    last = rows - (rows * DP * C - base)
    begin = last // 16 * 16
    for q in range(F):
        for who in range(DP):
            @pl.when(chips[who] == DP - 1)
            def _():
                extra_ref[q] = (
                    weight_ref[q, who, 0, C - 1, begin:size].astype(jnp.float32)
                    + weight_ref[q, who, 1, C - 1, begin:size].astype(jnp.float32)
                )
    pltpu.make_async_copy(table_ref.at[0], table_ref.at[0], gone_sem.at[0]).wait()
    for copy in blocks + sends:
        copy.wait_send()
    for q, who in ((0, 0),) + ORDER:
        always, inner = hops_of(q, who)
        for hop in always:
            copy_to(q, who, hop).wait_send()
        for hop in inner:
            pl.when(mid)(copy_to(q, who, hop).wait_send)


def tokens_kernel(
    sizes, state_ref, x_ref, extra_ref, same_ref,
    student_out, moment1_out, moment2_out, teacher_out, update_out, tokens_ref,
    stage_ref, sems, state_sems,
):
    DP, F, C = sizes
    f = lax.axis_index("fsdp")
    rows = state_ref.shape[1]
    patch_count = x_ref.shape[2]
    copies = []
    for number, target in enumerate((student_out, moment1_out, moment2_out, teacher_out, update_out)):
        copy = pltpu.make_async_copy(state_ref.at[number], target, state_sems.at[number])
        copy.start()
        copies.append(copy)
    mid = (f == 1) | (f == 2)
    away = jnp.where(f < 2, 1, -1)

    def place(i):
        inner = jnp.where(i == f, 0, jnp.where(i == f + away, 1, jnp.where(i == f - away, 2, 3)))
        return jnp.where(mid, inner, jnp.abs(i - f))

    places = [place(i) for i in range(F)]
    offset = (rows - 4) % 16

    def extra(n):
        return jnp.concatenate([extra_ref[at, offset + n : offset + n + 1] for at in places], axis=1)

    gain, shift = extra(2), extra(3)

    def normed(x):
        average = jnp.mean(x, axis=-1, keepdims=True)
        centered = x - average
        variance = jnp.mean(centered * centered, axis=-1, keepdims=True)
        return centered * lax.rsqrt(variance + norm_epsilon) * gain + shift

    class_row = normed(extra(0))
    for k in range(C):
        stage_ref[0:1, k] = class_row
    step = 32
    begun = 0
    picks = [jnp.broadcast_to(same_ref[k, 0:1, 0:1], (step, stage_ref.shape[2])) > 0.5 for k in range(C)]
    for number, start in enumerate(range(0, patch_count, step)):
        mine, other = (
            normed(jnp.concatenate([x_ref[at, k, start : start + step] for at in places], axis=1))
            for k in range(C)
        )
        for k in range(C):
            stage_ref[start + 1 : start + 1 + step, k] = jnp.where(picks[k], mine, other)
        end = start + 1 + step
        copy = pltpu.make_async_copy(
            stage_ref.at[begun:end], tokens_ref.at[begun:end], sems.at[number]
        )
        copy.start()
        copies.append(copy)
        begun = end
    for copy in copies:
        copy.wait()


def kernels(grad_parts, student, teacher, moment1, moment2, step_count, pixels, assign, sizes):
    DP, F, C = sizes
    rows, columns = student.shape
    spare = padded_rows(rows)
    slot = lanes_of(spare)
    own = pixels[0, 0].T
    pix_size, patch_count = own.shape
    here = pl.BlockSpec(memory_space=pltpu.VMEM)
    anywhere = pl.BlockSpec(memory_space=pl.ANY)
    scalars = pl.BlockSpec(memory_space=pltpu.SMEM)
    count = DP * C
    slab = spare - (rows - 4) // 16 * 16
    inputs = [
        pltpu.with_memory_space_constraint(value, pltpu.HBM)
        for value in (grad_parts, own, student, teacher, moment1, moment2, assign)
    ]
    shared = pl.pallas_call(
        functools.partial(refresh_kernel, sizes),
        out_shape=(
            pltpu.VMEM((5, rows, columns), jnp.float32),
            pltpu.VMEM((F, C, patch_count, columns), jnp.float32),
            pltpu.VMEM((F, slab, columns), jnp.float32),
            pltpu.VMEM((C, 8, 128), jnp.float32),
        ),
        in_specs=[anywhere] * 7 + [scalars],
        out_specs=(here,) * 4,
        scratch_shapes=[
            pltpu.VMEM((C, F, DP, spare, columns), jnp.int16),
            pltpu.VMEM((F, DP, 2, C, slot, columns), jnp.bfloat16),
            pltpu.VMEM((C, patch_count, count * 2 * slot), jnp.bfloat16),
            pltpu.VMEM((rows * (count - 1) + slot, patch_count), jnp.float32),
            pltpu.VMEM(own.shape, own.dtype),
            pltpu.VMEM(own.shape, own.dtype),
            pltpu.VMEM((DP, spare, columns), jnp.float32),
            pltpu.VMEM((DP, spare, columns), jnp.float32),
            pltpu.VMEM((DP, spare, columns), jnp.int16),
            pltpu.VMEM((DP, spare, columns), jnp.int16),
            pltpu.VMEM((spare, columns), jnp.float32),
            pltpu.VMEM((4, rows, columns), jnp.float32),
            pltpu.SMEM((1, C), jnp.int32),
            pltpu.SemaphoreType.DMA((6,)),
            pltpu.SemaphoreType.DMA((DP,)),
            pltpu.SemaphoreType.DMA((2, DP)),
            pltpu.SemaphoreType.DMA((DP,)),
            pltpu.SemaphoreType.DMA((DP,)),
            pltpu.SemaphoreType.DMA((2,)),
            pltpu.SemaphoreType.DMA((F, DP, OWN + F)),
            pltpu.SemaphoreType.DMA((F, DP)),
            pltpu.SemaphoreType.DMA((F, DP)),
            pltpu.SemaphoreType.DMA((1,)),
        ],
        compiler_params=pltpu.CompilerParams(
            collective_id=0, has_side_effects=True, vmem_limit_bytes=40 * 1024 * 1024
        ),
    )(*inputs, step_count)
    *results, tokens = pl.pallas_call(
        functools.partial(tokens_kernel, sizes),
        out_shape=(jax.ShapeDtypeStruct((rows, columns), jnp.float32),) * 5
        + (jax.ShapeDtypeStruct((patch_count + 1, C, columns * F), jnp.float32),),
        in_specs=[here] * 4,
        out_specs=(anywhere,) * 6,
        scratch_shapes=[
            pltpu.VMEM((patch_count + 1, C, columns * F), jnp.float32),
            pltpu.SemaphoreType.DMA((patch_count // 32,)),
            pltpu.SemaphoreType.DMA((5,)),
        ],
        compiler_params=pltpu.CompilerParams(vmem_limit_bytes=40 * 1024 * 1024),
    )(*(pltpu.with_memory_space_constraint(value, pltpu.VMEM) for value in shared))
    return (*results, tokens.transpose(1, 0, 2)[None])


def shards(grad_parts, student, teacher, moment1, moment2, step_count, pixels, assign):
    gradient = lax.psum_scatter(grad_parts[0], ("dp", "crop"), scatter_dimension=0, tiled=True)
    student_new, first_moment, second_moment, teacher_new, update = optimize(
        gradient, student, teacher, moment1, moment2, step_count
    )
    column_block = lax.all_gather(teacher_new, "fsdp", axis=1, tiled=True)
    gathered = lax.all_gather(column_block, ("dp", "crop"), axis=0, tiled=True)
    own_tokens = embed(pixels[:, 0], gathered)
    both = lax.all_gather(own_tokens[:, None], "crop", axis=1, tiled=True)
    teacher_tokens = jnp.where((assign == 0)[:, :, None, None], both[:, 0:1], both[:, 1:2])
    return (student_new, first_moment, second_moment, teacher_new, update, teacher_tokens)


def solution(mesh):
    placed = (
        P(("dp", "crop"), None, "fsdp"),
        P(("dp", "crop"), "fsdp"),
        P(("dp", "crop"), "fsdp"),
        P(("dp", "crop"), "fsdp"),
        P(("dp", "crop"), "fsdp"),
        P(),
        P(("dp", "fsdp"), "crop", None, None),
        P(("dp", "fsdp"), None),
    )
    sizes = (mesh.shape["dp"], mesh.shape["fsdp"], mesh.shape["crop"])

    def run(*args):
        grad_parts, student, pixels = args[0], args[1], args[6]
        fits = (
            student.shape[1] % 128 == 0
            and padded_rows(student.shape[0]) <= student.shape[1]
            and pixels.shape[:2] == (1, 1)
            and grad_parts.shape[0] == 1
            and sizes[0] == 4
            and sizes[1] == 4
            and pixels.shape[2] % 32 == 0
            and windows_fit(student.shape[0], sizes[0] * sizes[2])
            and sizes[2] == 2
        )
        return kernels(*args, sizes) if fits else shards(*args)

    return jax.shard_map(
        run,
        mesh=mesh,
        in_specs=placed,
        out_specs=(
            P(("dp", "crop"), "fsdp"),
            P(("dp", "crop"), "fsdp"),
            P(("dp", "crop"), "fsdp"),
            P(("dp", "crop"), "fsdp"),
            P(("dp", "crop"), "fsdp"),
            P(("dp", "fsdp"), None, None, None),
        ),
        check_vma=False,
    )
```

```python
import functools
import math

import jax
import jax.numpy as jnp
from jax import lax
from jax.experimental import pallas as pl
from jax.experimental.pallas import tpu as pltpu
from jax.sharding import PartitionSpec as P

beta_one = 0.9
beta_two = 0.999
adam_epsilon = 1e-08
learn_rate = 0.001
weight_decay = 0.04
momentum_base = 0.992
plan_length = 625000.0
norm_epsilon = 1e-06


def optimize(gradient, student, teacher, moment1, moment2, step_count):
    step_value = step_count[0].astype(jnp.float32)
    first_moment = beta_one * moment1 + (1.0 - beta_one) * gradient
    second_moment = beta_two * moment2 + (1.0 - beta_two) * gradient * gradient
    first_fix = 1.0 - jnp.power(jnp.float32(beta_one), step_value)
    second_fix = 1.0 - jnp.power(jnp.float32(beta_two), step_value)
    update = (
        first_moment / first_fix / (jnp.sqrt(second_moment / second_fix) + adam_epsilon)
        + weight_decay * student
    )
    student_new = student - learn_rate * update
    momentum = (
        1.0 - (1.0 - momentum_base) * (jnp.cos(math.pi * step_value / plan_length) + 1.0) / 2.0
    )
    teacher_new = momentum * teacher + (1.0 - momentum) * student_new
    return (student_new, first_moment, second_moment, teacher_new, update)


def embed(patches, table):
    count = patches.shape[0]
    pix_size = patches.shape[2]
    patch_count = patches.shape[1]
    width = table.shape[1]
    weight = table[:pix_size]
    position = table[pix_size : pix_size + patch_count]
    extras = table[pix_size + patch_count :]
    flat_patches = patches.reshape(count * patch_count, pix_size).astype(jnp.float32)
    projected = jnp.dot(
        flat_patches, weight, precision=lax.Precision.HIGHEST, preferred_element_type=jnp.float32
    )
    projected = projected.reshape(count, patch_count, width) + extras[1] + position
    class_row = jnp.broadcast_to(extras[0], (count, 1, width))
    tokens = jnp.concatenate([class_row, projected], axis=1)
    average = jnp.mean(tokens, axis=-1, keepdims=True)
    centered = tokens - average
    variance = jnp.mean(centered * centered, axis=-1, keepdims=True)
    return centered * lax.rsqrt(variance + norm_epsilon) * extras[2] + extras[3]


LEVELS = 32767.0
CODES = 256.0
MESH = pl.DeviceIdType.MESH


def padded_rows(rows):
    return -(-(rows + 1) // 16) * 16


def lanes_of(count):
    return -(-count // 128) * 128


def windows_fit(rows, count):
    size = padded_rows(rows)
    return all(j * rows % 8 + rows <= size and j * rows // 8 * 8 + size <= rows * count for j in range(count))


def turned(count, width, offset):
    row = lax.broadcasted_iota(jnp.int32, (count, width), 0) - offset
    return jnp.where(row < 0, row + count, row)


def encode(value, rows, offset):
    count, width = value.shape
    row_index = turned(count, width, offset)
    value = jnp.where(row_index < rows, value, 0.0)
    top = jnp.maximum(jnp.max(jnp.abs(value), axis=1, keepdims=True), 1e-30)
    code = jnp.ceil(jnp.log2(top) * CODES + 0.01)
    scaled = value * (jnp.exp2(code * (-1.0 / CODES)) * LEVELS)
    lanes = lanes_of(count)
    lane = lax.broadcasted_iota(jnp.int32, (count, lanes), 1)
    near = jnp.where(row_index[:, :lanes] == lane, code, 0.0)
    code_row = jnp.sum(near, axis=0, keepdims=True)
    if width > lanes:
        rest = jnp.zeros((1, width - lanes), jnp.float32)
        code_row = jnp.concatenate([code_row, rest], axis=1)
    out = jnp.where(row_index == rows, jnp.broadcast_to(code_row, (count, width)), scaled)
    out = jnp.clip(jnp.round(out), -LEVELS, LEVELS)
    return out.astype(jnp.int32).astype(jnp.int16)


def decode(block, rows, offset):
    count, width = block.shape
    value = block.astype(jnp.int32).astype(jnp.float32)
    lanes = lanes_of(count)
    lane = lax.broadcasted_iota(jnp.int32, (count, lanes), 1)
    row_index = turned(count, lanes, offset)
    if isinstance(offset, int):
        code_row = value[rows : rows + 1, :lanes]
    else:
        code_row = jnp.sum(jnp.where(row_index == rows, value[:, :lanes], 0.0), axis=0, keepdims=True)
    near = jnp.where(row_index == lane, code_row, 0.0)
    code = jnp.sum(near, axis=1, keepdims=True)
    return value * (jnp.exp2(code * (1.0 / CODES)) * (1.0 / LEVELS))


OWN = 4
ORDER = (
    (1, 0), (0, 1), (0, 2), (2, 0), (3, 0), (0, 3), (1, 1), (1, 3), (1, 2), (2, 1), (2, 2),
    (3, 1), (3, 2), (2, 3), (3, 3),
)
GROUPS = ((0, 1, 2), (3,))
LAG = 2
ARRIVE = (1, 2, 0)


def schedule(step_ref):
    step_value = jnp.full((8, 128), step_ref[0], jnp.int32).astype(jnp.float32)
    first_fix = 1.0 - jnp.power(jnp.full((8, 128), beta_one, jnp.float32), step_value)
    second_fix = 1.0 - jnp.power(jnp.full((8, 128), beta_two, jnp.float32), step_value)
    momentum = (
        1.0 - (1.0 - momentum_base) * (jnp.cos(math.pi * step_value / plan_length) + 1.0) / 2.0
    )
    return first_fix[0:1, 0:1], second_fix[0:1, 0:1], momentum[0:1, 0:1]


def step_of(gradient, student, teacher, moment1, moment2, step_ref):
    first_fix, second_fix, momentum = schedule(step_ref)
    first_moment = beta_one * moment1 + (1.0 - beta_one) * gradient
    second_moment = beta_two * moment2 + (1.0 - beta_two) * gradient * gradient
    update = (
        first_moment / first_fix / (jnp.sqrt(second_moment / second_fix) + adam_epsilon)
        + weight_decay * student
    )
    student_new = student - learn_rate * update
    teacher_new = momentum * teacher + (1.0 - momentum) * student_new
    return student_new, first_moment, second_moment, teacher_new, update


def hops_of(q, who):
    if who == 0:
        along = (OWN + 1, OWN + 3, OWN + 2) if q == 0 else ()
        return along + ((3,) if q in (0, 3) else ()) + (1, 2), ()
    if who == 3 and q == 0:
        return (OWN + 1,), (OWN + 2,)
    if who == 3 and q == 1:
        return (), (OWN + 2,)
    return (), ()


def refresh_kernel(
    sizes, grad_ref, pixel_ref, student_ref, teacher_ref, moment1_ref, moment2_ref, pick_ref, step_ref,
    state_ref, x_ref, extra_ref, same_ref,
    table_ref, weight_ref, left_ref, pixels_ref, mine_ref, other_ref, half_ref, pre_ref, out_ref, in_ref,
    space_ref, held_ref, pick_now,
    load_sem, half_sem, pair_sem, out_sem, in_sem, pix_sem, go_sem, come_sem, share_sem, gone_sem,
):
    DP, F, C = sizes
    rows, size = student_ref.shape[0], table_ref.shape[3]
    d, f, c = lax.axis_index("dp"), lax.axis_index("fsdp"), lax.axis_index("crop")
    partner = lax.rem(c + 1, C)

    barrier = pltpu.get_barrier_semaphore()
    pl.semaphore_signal(barrier, inc=1, device_id={"crop": partner}, device_id_type=MESH)
    for r in range(1, DP):
        pl.semaphore_signal(barrier, inc=1, device_id={"dp": lax.rem(d + r, DP)}, device_id_type=MESH)
    for r in range(1, F):
        pl.semaphore_signal(barrier, inc=1, device_id={"fsdp": lax.rem(f + r, F)}, device_id_type=MESH)

    row, column = d // 2, lax.rem(d, 2)
    chips = (
        d,
        row * 2 + 1 - column,
        (1 - row) * 2 + column,
        (1 - row) * 2 + 1 - column,
    )
    order = (3, 1, 2, 0)

    def window(at, core):
        start = (at * C + core) * rows // 8 * 8
        return grad_ref.at[0, pl.ds(pl.multiple_of(start, 8), size)]

    halves = []
    for r in order:
        copy = pltpu.make_async_copy(window(chips[r], c), half_ref.at[r], half_sem.at[r])
        copy.start()
        halves.append(copy)
    loads = []
    for source, target in (
        (pick_ref, pick_now), (pixel_ref, mine_ref), (student_ref, held_ref.at[0]),
        (teacher_ref, held_ref.at[1]), (moment1_ref, held_ref.at[2]), (moment2_ref, held_ref.at[3]),
    ):
        copy = pltpu.make_async_copy(source, target, load_sem.at[len(loads)])
        copy.start()
        loads.append(copy)

    pl.semaphore_wait(barrier, DP - 1 + 1 + F - 1)
    sends = []
    for r in order:
        copy = pltpu.make_async_remote_copy(
            src_ref=window(chips[r], partner), dst_ref=pre_ref.at[r],
            send_sem=pair_sem.at[0, r], recv_sem=pair_sem.at[1, r],
            device_id={"crop": partner}, device_id_type=MESH,
        )
        copy.start()
        sends.append(copy)
    blocks = []
    total = None
    offset = (d * C + c) * rows % 8
    for number, r in enumerate(order):
        at = chips[r]
        halves[number].wait()
        sends[number].wait_recv()
        chip = half_ref[r] + pre_ref[r]
        if r == 0:
            total = chip
            break
        out_ref[r] = encode(chip, rows, (at * C + c) * rows % 8)
        copy = pltpu.make_async_remote_copy(
            src_ref=out_ref.at[r], dst_ref=in_ref.at[r],
            send_sem=out_sem.at[r], recv_sem=in_sem.at[r],
            device_id={"dp": at}, device_id_type=MESH,
        )
        copy.start()
        blocks.append(copy)
    pixel_copy = pltpu.make_async_remote_copy(
        src_ref=pixel_ref, dst_ref=other_ref, send_sem=pix_sem.at[0], recv_sem=pix_sem.at[1],
        device_id={"crop": partner}, device_id_type=MESH,
    )
    pixel_copy.start()
    for copy in loads:
        copy.wait()

    slot = weight_ref.shape[4]
    depth = 2 * C * slot
    pix_size, patch_count = pixel_ref.shape
    base = pix_size + patch_count

    def prepare(k, source_ref):
        pixels_ref[0:pix_size] = source_ref[...].astype(jnp.float32)
        pixels_ref[pix_size:] = jnp.zeros((pixels_ref.shape[0] - pix_size, patch_count), jnp.float32)
        for j in range(DP * C):
            lane = lax.broadcasted_iota(jnp.int32, (patch_count, slot), 1)
            patch = lax.broadcasted_iota(jnp.int32, (patch_count, slot), 0)
            at = lane + j * rows
            inside = lane < rows
            one = inside & ((at == base + 1) | ((at < base) & (at - pix_size == patch)))
            block = jnp.where(one, 1.0, 0.0)
            if j * rows < pix_size:
                block = block + jnp.where(inside, pixels_ref[j * rows : j * rows + slot].T, 0.0)
            near = lax.rem(j // C // 2 + row, 2) * 2 + lax.rem(j // C + column, 2)
            block = block.astype(jnp.bfloat16)
            for level in range(2):
                start = near * depth + (level * C + j % C) * slot
                left_ref[k, :, pl.ds(pl.multiple_of(start, 128), slot)] = block

    blank = jnp.zeros((F, DP, 2, C, slot - size, weight_ref.shape[5]), jnp.bfloat16)
    weight_ref[:, :, :, :, size:] = blank
    prepare(0, mine_ref)
    for k in range(C):
        same_ref[0, k] = jnp.where(pick_now[0, k] == c, 0, 1)
    for number in ARRIVE:
        blocks[number].wait_recv()
        total = total + decode(in_ref[order[number]], rows, offset)
    gradient = pltpu.roll(total, lax.rem(size - offset, size), 0)[0:rows]
    fresh = step_of(gradient, held_ref[0], held_ref[1], held_ref[2], held_ref[3], step_ref)
    space_ref[rows:] = jnp.zeros((size - rows, space_ref.shape[1]), jnp.float32)
    space_ref[0:rows] = fresh[3]
    table_ref[0, 0, 0] = encode(space_ref[...], rows, 0)

    mid = (f == 1) | (f == 2)
    away = jnp.where(f < 2, 1, -1)
    planes = (
        f,
        f + away,
        jnp.where(mid, f - away, f + 2 * away),
        jnp.where(mid, f + 2 * away, f + 3 * away),
    )
    slots = (0, jnp.where(mid, 1, 2), jnp.where(mid, 1, 3), jnp.where(mid, 2, 3))

    def copy_to(q, who, hop):
        if hop < OWN:
            to, there = {"dp": chips[hop]}, (q, who ^ hop)
        else:
            to = {"fsdp": planes[hop - OWN]}
            there = (slots[hop - OWN] if q == 0 else 2, who)
        return pltpu.make_async_remote_copy(
            src_ref=table_ref.at[0, q, who], dst_ref=table_ref.at[(0, *there)],
            send_sem=go_sem.at[q, who, hop], recv_sem=come_sem.at[there],
            device_id=to, device_id_type=MESH,
        )

    def pass_on(q, who):
        always, inner = hops_of(q, who)
        for hop in always:
            copy_to(q, who, hop).start()
        for hop in inner:
            pl.when(mid)(copy_to(q, who, hop).start)
        pltpu.make_async_remote_copy(
            src_ref=table_ref.at[0, q, who], dst_ref=table_ref.at[1, q, who],
            send_sem=gone_sem.at[0], recv_sem=share_sem.at[q, who],
            device_id={"crop": partner}, device_id_type=MESH,
        ).start()

    def arrive(core, q, who):
        block = table_ref.at[core, q, who]
        sem = share_sem.at[q, who] if core else come_sem.at[q, who]
        pltpu.make_async_copy(block, block, sem).wait()

    def unpack(core, q, who):
        value = decode(table_ref[core, q, who], rows, 0)
        high = value.astype(jnp.bfloat16)
        place = (c, partner)[core]
        weight_ref[q, who, 0, place, 0:size] = high
        weight_ref[q, who, 1, place, 0:size] = (value - high.astype(jnp.float32)).astype(jnp.bfloat16)

    started = set()

    def multiply(q, group):
        first, last = group[0], group[-1] + 1
        right = weight_ref[q, first:last].reshape((last - first) * depth, weight_ref.shape[5])
        for k in range(C):
            left = left_ref[k, :, first * depth : last * depth]
            now = jnp.dot(left, right, preferred_element_type=jnp.float32)
            x_ref[q, k] = x_ref[q, k] + now if q in started else now
        started.add(q)

    pass_on(0, 0)
    for number in range(5):
        state_ref[number] = fresh[number]
    pixel_copy.wait()
    prepare(1, other_ref)
    seen = set()

    def finish(q, who):
        arrive(1, q, who)
        unpack(1, q, who)
        seen.add((q, who))
        for group in GROUPS:
            if who in group and all((q, other) in seen for other in group):
                multiply(q, group)

    unpack(0, 0, 0)
    ready = [(0, 0)]
    for q, who in ORDER:
        arrive(0, q, who)
        pass_on(q, who)
        unpack(0, q, who)
        ready.append((q, who))
        if len(ready) > LAG:
            finish(*ready.pop(0))
    for q, who in ready:
        finish(q, who)
    last = rows - (rows * DP * C - base)
    begin = last // 16 * 16
    for q in range(F):
        for who in range(DP):
            @pl.when(chips[who] == DP - 1)
            def _():
                extra_ref[q] = (
                    weight_ref[q, who, 0, C - 1, begin:size].astype(jnp.float32)
                    + weight_ref[q, who, 1, C - 1, begin:size].astype(jnp.float32)
                )
    pltpu.make_async_copy(table_ref.at[0], table_ref.at[0], gone_sem.at[0]).wait()
    for copy in blocks + sends:
        copy.wait_send()
    for q, who in ((0, 0),) + ORDER:
        always, inner = hops_of(q, who)
        for hop in always:
            copy_to(q, who, hop).wait_send()
        for hop in inner:
            pl.when(mid)(copy_to(q, who, hop).wait_send)


def tokens_kernel(
    sizes, state_ref, x_ref, extra_ref, same_ref,
    student_out, moment1_out, moment2_out, teacher_out, update_out, tokens_ref,
    stage_ref, sems, state_sems,
):
    DP, F, C = sizes
    f = lax.axis_index("fsdp")
    rows = state_ref.shape[1]
    patch_count = x_ref.shape[2]
    copies = []
    for number, target in enumerate((student_out, moment1_out, moment2_out, teacher_out, update_out)):
        copy = pltpu.make_async_copy(state_ref.at[number], target, state_sems.at[number])
        copy.start()
        copies.append(copy)
    mid = (f == 1) | (f == 2)
    away = jnp.where(f < 2, 1, -1)

    def place(i):
        inner = jnp.where(i == f, 0, jnp.where(i == f + away, 1, jnp.where(i == f - away, 2, 3)))
        return jnp.where(mid, inner, jnp.abs(i - f))

    places = [place(i) for i in range(F)]
    offset = (rows - 4) % 16

    def extra(n):
        return jnp.concatenate([extra_ref[at, offset + n : offset + n + 1] for at in places], axis=1)

    gain, shift = extra(2), extra(3)

    def normed(x):
        average = jnp.mean(x, axis=-1, keepdims=True)
        centered = x - average
        variance = jnp.mean(centered * centered, axis=-1, keepdims=True)
        return centered * lax.rsqrt(variance + norm_epsilon) * gain + shift

    class_row = normed(extra(0))
    for k in range(C):
        stage_ref[0:1, k] = class_row
    step = 32
    begun = 0
    for number, start in enumerate(range(0, patch_count, step)):
        for k in range(C):
            source = same_ref[0, k]
            x = jnp.concatenate([x_ref[at, source, start : start + step] for at in places], axis=1)
            stage_ref[start + 1 : start + 1 + step, k] = normed(x)
        end = start + 1 + step
        copy = pltpu.make_async_copy(
            stage_ref.at[begun:end], tokens_ref.at[begun:end], sems.at[number]
        )
        copy.start()
        copies.append(copy)
        begun = end
    for copy in copies:
        copy.wait()


def kernels(grad_parts, student, teacher, moment1, moment2, step_count, pixels, assign, sizes):
    DP, F, C = sizes
    rows, columns = student.shape
    spare = padded_rows(rows)
    slot = lanes_of(spare)
    own = pixels[0, 0].T
    pix_size, patch_count = own.shape
    here = pl.BlockSpec(memory_space=pltpu.VMEM)
    anywhere = pl.BlockSpec(memory_space=pl.ANY)
    scalars = pl.BlockSpec(memory_space=pltpu.SMEM)
    count = DP * C
    slab = spare - (rows - 4) // 16 * 16
    inputs = [
        pltpu.with_memory_space_constraint(value, pltpu.HBM)
        for value in (grad_parts, own, student, teacher, moment1, moment2, assign)
    ]
    shared = pl.pallas_call(
        functools.partial(refresh_kernel, sizes),
        out_shape=(
            pltpu.VMEM((5, rows, columns), jnp.float32),
            pltpu.VMEM((F, C, patch_count, columns), jnp.float32),
            pltpu.VMEM((F, slab, columns), jnp.float32),
            pltpu.SMEM((1, C), jnp.int32),
        ),
        in_specs=[anywhere] * 7 + [scalars],
        out_specs=(here,) * 3 + (scalars,),
        scratch_shapes=[
            pltpu.VMEM((C, F, DP, spare, columns), jnp.int16),
            pltpu.VMEM((F, DP, 2, C, slot, columns), jnp.bfloat16),
            pltpu.VMEM((C, patch_count, count * 2 * slot), jnp.bfloat16),
            pltpu.VMEM((rows * (count - 1) + slot, patch_count), jnp.float32),
            pltpu.VMEM(own.shape, own.dtype),
            pltpu.VMEM(own.shape, own.dtype),
            pltpu.VMEM((DP, spare, columns), jnp.float32),
            pltpu.VMEM((DP, spare, columns), jnp.float32),
            pltpu.VMEM((DP, spare, columns), jnp.int16),
            pltpu.VMEM((DP, spare, columns), jnp.int16),
            pltpu.VMEM((spare, columns), jnp.float32),
            pltpu.VMEM((4, rows, columns), jnp.float32),
            pltpu.SMEM((1, C), jnp.int32),
            pltpu.SemaphoreType.DMA((6,)),
            pltpu.SemaphoreType.DMA((DP,)),
            pltpu.SemaphoreType.DMA((2, DP)),
            pltpu.SemaphoreType.DMA((DP,)),
            pltpu.SemaphoreType.DMA((DP,)),
            pltpu.SemaphoreType.DMA((2,)),
            pltpu.SemaphoreType.DMA((F, DP, OWN + F)),
            pltpu.SemaphoreType.DMA((F, DP)),
            pltpu.SemaphoreType.DMA((F, DP)),
            pltpu.SemaphoreType.DMA((1,)),
        ],
        compiler_params=pltpu.CompilerParams(
            collective_id=0, has_side_effects=True, vmem_limit_bytes=40 * 1024 * 1024
        ),
    )(*inputs, step_count)
    *results, tokens = pl.pallas_call(
        functools.partial(tokens_kernel, sizes),
        out_shape=(jax.ShapeDtypeStruct((rows, columns), jnp.float32),) * 5
        + (jax.ShapeDtypeStruct((patch_count + 1, C, columns * F), jnp.float32),),
        in_specs=[here] * 3 + [scalars],
        out_specs=(anywhere,) * 6,
        scratch_shapes=[
            pltpu.VMEM((patch_count + 1, C, columns * F), jnp.float32),
            pltpu.SemaphoreType.DMA((patch_count // 32,)),
            pltpu.SemaphoreType.DMA((5,)),
        ],
        compiler_params=pltpu.CompilerParams(vmem_limit_bytes=40 * 1024 * 1024),
    )(*(pltpu.with_memory_space_constraint(value, pltpu.VMEM) for value in shared[:3]), shared[3])
    return (*results, tokens.transpose(1, 0, 2)[None])


def shards(grad_parts, student, teacher, moment1, moment2, step_count, pixels, assign):
    gradient = lax.psum_scatter(grad_parts[0], ("dp", "crop"), scatter_dimension=0, tiled=True)
    student_new, first_moment, second_moment, teacher_new, update = optimize(
        gradient, student, teacher, moment1, moment2, step_count
    )
    column_block = lax.all_gather(teacher_new, "fsdp", axis=1, tiled=True)
    gathered = lax.all_gather(column_block, ("dp", "crop"), axis=0, tiled=True)
    own_tokens = embed(pixels[:, 0], gathered)
    both = lax.all_gather(own_tokens[:, None], "crop", axis=1, tiled=True)
    teacher_tokens = jnp.where((assign == 0)[:, :, None, None], both[:, 0:1], both[:, 1:2])
    return (student_new, first_moment, second_moment, teacher_new, update, teacher_tokens)


def solution(mesh):
    placed = (
        P(("dp", "crop"), None, "fsdp"),
        P(("dp", "crop"), "fsdp"),
        P(("dp", "crop"), "fsdp"),
        P(("dp", "crop"), "fsdp"),
        P(("dp", "crop"), "fsdp"),
        P(),
        P(("dp", "fsdp"), "crop", None, None),
        P(("dp", "fsdp"), None),
    )
    sizes = (mesh.shape["dp"], mesh.shape["fsdp"], mesh.shape["crop"])

    def run(*args):
        grad_parts, student, pixels = args[0], args[1], args[6]
        fits = (
            student.shape[1] % 128 == 0
            and padded_rows(student.shape[0]) <= student.shape[1]
            and pixels.shape[:2] == (1, 1)
            and grad_parts.shape[0] == 1
            and sizes[0] == 4
            and sizes[1] == 4
            and pixels.shape[2] % 32 == 0
            and windows_fit(student.shape[0], sizes[0] * sizes[2])
            and sizes[2] == 2
        )
        return kernels(*args, sizes) if fits else shards(*args)

    return jax.shard_map(
        run,
        mesh=mesh,
        in_specs=placed,
        out_specs=(
            P(("dp", "crop"), "fsdp"),
            P(("dp", "crop"), "fsdp"),
            P(("dp", "crop"), "fsdp"),
            P(("dp", "crop"), "fsdp"),
            P(("dp", "crop"), "fsdp"),
            P(("dp", "fsdp"), None, None, None),
        ),
        check_vma=False,
    )
```

```python
import functools
import math

import jax
import jax.numpy as jnp
from jax import lax
from jax.experimental import pallas as pl
from jax.experimental.pallas import tpu as pltpu
from jax.sharding import PartitionSpec as P

beta_one = 0.9
beta_two = 0.999
adam_epsilon = 1e-08
learn_rate = 0.001
weight_decay = 0.04
momentum_base = 0.992
plan_length = 625000.0
norm_epsilon = 1e-06


def optimize(gradient, student, teacher, moment1, moment2, step_count):
    step_value = step_count[0].astype(jnp.float32)
    first_moment = beta_one * moment1 + (1.0 - beta_one) * gradient
    second_moment = beta_two * moment2 + (1.0 - beta_two) * gradient * gradient
    first_fix = 1.0 - jnp.power(jnp.float32(beta_one), step_value)
    second_fix = 1.0 - jnp.power(jnp.float32(beta_two), step_value)
    update = (
        first_moment / first_fix / (jnp.sqrt(second_moment / second_fix) + adam_epsilon)
        + weight_decay * student
    )
    student_new = student - learn_rate * update
    momentum = (
        1.0 - (1.0 - momentum_base) * (jnp.cos(math.pi * step_value / plan_length) + 1.0) / 2.0
    )
    teacher_new = momentum * teacher + (1.0 - momentum) * student_new
    return (student_new, first_moment, second_moment, teacher_new, update)


def embed(patches, table):
    count = patches.shape[0]
    pix_size = patches.shape[2]
    patch_count = patches.shape[1]
    width = table.shape[1]
    weight = table[:pix_size]
    position = table[pix_size : pix_size + patch_count]
    extras = table[pix_size + patch_count :]
    flat_patches = patches.reshape(count * patch_count, pix_size).astype(jnp.float32)
    projected = jnp.dot(
        flat_patches, weight, precision=lax.Precision.HIGHEST, preferred_element_type=jnp.float32
    )
    projected = projected.reshape(count, patch_count, width) + extras[1] + position
    class_row = jnp.broadcast_to(extras[0], (count, 1, width))
    tokens = jnp.concatenate([class_row, projected], axis=1)
    average = jnp.mean(tokens, axis=-1, keepdims=True)
    centered = tokens - average
    variance = jnp.mean(centered * centered, axis=-1, keepdims=True)
    return centered * lax.rsqrt(variance + norm_epsilon) * extras[2] + extras[3]


LEVELS = 32767.0
CODES = 256.0
MESH = pl.DeviceIdType.MESH


def padded_rows(rows):
    return -(-(rows + 1) // 16) * 16


def lanes_of(count):
    return -(-count // 128) * 128


def windows_fit(rows, count):
    size = padded_rows(rows)
    return all(j * rows % 8 + rows <= size and j * rows // 8 * 8 + size <= rows * count for j in range(count))


def turned(count, width, offset):
    row = lax.broadcasted_iota(jnp.int32, (count, width), 0) - offset
    return jnp.where(row < 0, row + count, row)


def encode(value, rows, offset):
    count, width = value.shape
    row_index = turned(count, width, offset)
    value = jnp.where(row_index < rows, value, 0.0)
    top = jnp.maximum(jnp.max(jnp.abs(value), axis=1, keepdims=True), 1e-30)
    code = jnp.ceil(jnp.log2(top) * CODES + 0.01)
    scaled = value * (jnp.exp2(code * (-1.0 / CODES)) * LEVELS)
    lanes = lanes_of(count)
    lane = lax.broadcasted_iota(jnp.int32, (count, lanes), 1)
    near = jnp.where(row_index[:, :lanes] == lane, code, 0.0)
    code_row = jnp.sum(near, axis=0, keepdims=True)
    if width > lanes:
        rest = jnp.zeros((1, width - lanes), jnp.float32)
        code_row = jnp.concatenate([code_row, rest], axis=1)
    out = jnp.where(row_index == rows, jnp.broadcast_to(code_row, (count, width)), scaled)
    out = jnp.clip(jnp.round(out), -LEVELS, LEVELS)
    return out.astype(jnp.int32).astype(jnp.int16)


def decode(block, rows, offset):
    count, width = block.shape
    value = block.astype(jnp.int32).astype(jnp.float32)
    lanes = lanes_of(count)
    lane = lax.broadcasted_iota(jnp.int32, (count, lanes), 1)
    row_index = turned(count, lanes, offset)
    if isinstance(offset, int):
        code_row = value[rows : rows + 1, :lanes]
    else:
        code_row = jnp.sum(jnp.where(row_index == rows, value[:, :lanes], 0.0), axis=0, keepdims=True)
    near = jnp.where(row_index == lane, code_row, 0.0)
    code = jnp.sum(near, axis=1, keepdims=True)
    return value * (jnp.exp2(code * (1.0 / CODES)) * (1.0 / LEVELS))


OWN = 4
ORDER = (
    (1, 0), (0, 1), (0, 2), (2, 0), (3, 0), (0, 3), (1, 1), (1, 3), (1, 2), (2, 1), (2, 2),
    (3, 1), (3, 2), (2, 3), (3, 3),
)
GROUPS = (
    ((0, 1), (0, 1, 2)), ((0, 1), (3,)), ((2, 3), (0, 1, 2)), ((2, 3), (3,)),
)
LAG = 2
ARRIVE = (1, 2, 0)


def schedule(step_ref):
    step_value = jnp.full((8, 128), step_ref[0], jnp.int32).astype(jnp.float32)
    first_fix = 1.0 - jnp.power(jnp.full((8, 128), beta_one, jnp.float32), step_value)
    second_fix = 1.0 - jnp.power(jnp.full((8, 128), beta_two, jnp.float32), step_value)
    momentum = (
        1.0 - (1.0 - momentum_base) * (jnp.cos(math.pi * step_value / plan_length) + 1.0) / 2.0
    )
    return first_fix[0:1, 0:1], second_fix[0:1, 0:1], momentum[0:1, 0:1]


def step_of(gradient, student, teacher, moment1, moment2, step_ref):
    first_fix, second_fix, momentum = schedule(step_ref)
    first_moment = beta_one * moment1 + (1.0 - beta_one) * gradient
    second_moment = beta_two * moment2 + (1.0 - beta_two) * gradient * gradient
    update = (
        first_moment / first_fix / (jnp.sqrt(second_moment / second_fix) + adam_epsilon)
        + weight_decay * student
    )
    student_new = student - learn_rate * update
    teacher_new = momentum * teacher + (1.0 - momentum) * student_new
    return student_new, first_moment, second_moment, teacher_new, update


def hops_of(q, who):
    if who == 0:
        along = (OWN + 1, OWN + 3, OWN + 2) if q == 0 else ()
        return along + ((3,) if q in (0, 3) else ()) + (1, 2), ()
    if who == 3 and q == 0:
        return (OWN + 1,), (OWN + 2,)
    if who == 3 and q == 1:
        return (), (OWN + 2,)
    return (), ()


def refresh_kernel(
    sizes, grad_ref, pixel_ref, student_ref, teacher_ref, moment1_ref, moment2_ref, pick_ref, step_ref,
    state_ref, x_ref, extra_ref, same_ref,
    table_ref, weight_ref, left_ref, pixels_ref, mine_ref, other_ref, half_ref, pre_ref, out_ref, in_ref,
    space_ref, held_ref, pick_now,
    load_sem, half_sem, pair_sem, out_sem, in_sem, pix_sem, go_sem, come_sem, share_sem, gone_sem,
):
    DP, F, C = sizes
    (rows, columns), size = student_ref.shape, table_ref.shape[3]
    d, f, c = lax.axis_index("dp"), lax.axis_index("fsdp"), lax.axis_index("crop")
    partner = lax.rem(c + 1, C)

    barrier = pltpu.get_barrier_semaphore()
    pl.semaphore_signal(barrier, inc=1, device_id={"crop": partner}, device_id_type=MESH)
    for r in range(1, DP):
        pl.semaphore_signal(barrier, inc=1, device_id={"dp": lax.rem(d + r, DP)}, device_id_type=MESH)
    for r in range(1, F):
        pl.semaphore_signal(barrier, inc=1, device_id={"fsdp": lax.rem(f + r, F)}, device_id_type=MESH)

    row, column = d // 2, lax.rem(d, 2)
    chips = (
        d,
        row * 2 + 1 - column,
        (1 - row) * 2 + column,
        (1 - row) * 2 + 1 - column,
    )
    order = (3, 1, 2, 0)

    def window(at, core):
        start = (at * C + core) * rows // 8 * 8
        return grad_ref.at[0, pl.ds(pl.multiple_of(start, 8), size)]

    halves = []
    for r in order:
        copy = pltpu.make_async_copy(window(chips[r], c), half_ref.at[r], half_sem.at[r])
        copy.start()
        halves.append(copy)
    loads = []
    for source, target in (
        (pick_ref, pick_now), (pixel_ref, mine_ref), (student_ref, held_ref.at[0]),
        (teacher_ref, held_ref.at[1]), (moment1_ref, held_ref.at[2]), (moment2_ref, held_ref.at[3]),
    ):
        copy = pltpu.make_async_copy(source, target, load_sem.at[len(loads)])
        copy.start()
        loads.append(copy)

    pl.semaphore_wait(barrier, DP - 1 + 1 + F - 1)
    sends = []
    for r in order:
        copy = pltpu.make_async_remote_copy(
            src_ref=window(chips[r], partner), dst_ref=pre_ref.at[r],
            send_sem=pair_sem.at[0, r], recv_sem=pair_sem.at[1, r],
            device_id={"crop": partner}, device_id_type=MESH,
        )
        copy.start()
        sends.append(copy)
    blocks = []
    total = None
    offset = (d * C + c) * rows % 8
    for number, r in enumerate(order):
        at = chips[r]
        halves[number].wait()
        sends[number].wait_recv()
        chip = half_ref[r] + pre_ref[r]
        if r == 0:
            total = chip
            break
        out_ref[r] = encode(chip, rows, (at * C + c) * rows % 8)
        copy = pltpu.make_async_remote_copy(
            src_ref=out_ref.at[r], dst_ref=in_ref.at[r],
            send_sem=out_sem.at[r], recv_sem=in_sem.at[r],
            device_id={"dp": at}, device_id_type=MESH,
        )
        copy.start()
        blocks.append(copy)
    pixel_copy = pltpu.make_async_remote_copy(
        src_ref=pixel_ref, dst_ref=other_ref, send_sem=pix_sem.at[0], recv_sem=pix_sem.at[1],
        device_id={"crop": partner}, device_id_type=MESH,
    )
    pixel_copy.start()
    for copy in loads:
        copy.wait()

    slot = weight_ref.shape[4]
    depth = 2 * C * slot
    pix_size, patch_count = pixel_ref.shape
    base = pix_size + patch_count

    def prepare(k, source_ref):
        pixels_ref[0:pix_size] = source_ref[...].astype(jnp.float32)
        pixels_ref[pix_size:] = jnp.zeros((pixels_ref.shape[0] - pix_size, patch_count), jnp.float32)
        for j in range(DP * C):
            lane = lax.broadcasted_iota(jnp.int32, (patch_count, slot), 1)
            patch = lax.broadcasted_iota(jnp.int32, (patch_count, slot), 0)
            at = lane + j * rows
            inside = lane < rows
            one = inside & ((at == base + 1) | ((at < base) & (at - pix_size == patch)))
            block = jnp.where(one, 1.0, 0.0)
            if j * rows < pix_size:
                block = block + jnp.where(inside, pixels_ref[j * rows : j * rows + slot].T, 0.0)
            near = lax.rem(j // C // 2 + row, 2) * 2 + lax.rem(j // C + column, 2)
            block = block.astype(jnp.bfloat16)
            for level in range(2):
                start = near * depth + (level * C + j % C) * slot
                left_ref[k, :, pl.ds(pl.multiple_of(start, 128), slot)] = block

    blank = jnp.zeros((F // 2, DP, 2, C, slot - size, weight_ref.shape[5]), jnp.bfloat16)
    weight_ref[:, :, :, :, size:] = blank
    prepare(0, mine_ref)
    for k in range(C):
        same_ref[0, k] = jnp.where(pick_now[0, k] == c, 0, 1)
    for number in ARRIVE:
        blocks[number].wait_recv()
        total = total + decode(in_ref[order[number]], rows, offset)
    gradient = pltpu.roll(total, lax.rem(size - offset, size), 0)[0:rows]
    fresh = step_of(gradient, held_ref[0], held_ref[1], held_ref[2], held_ref[3], step_ref)
    space_ref[rows:] = jnp.zeros((size - rows, space_ref.shape[1]), jnp.float32)
    space_ref[0:rows] = fresh[3]
    table_ref[0, 0, 0] = encode(space_ref[...], rows, 0)

    mid = (f == 1) | (f == 2)
    away = jnp.where(f < 2, 1, -1)
    planes = (
        f,
        f + away,
        jnp.where(mid, f - away, f + 2 * away),
        jnp.where(mid, f + 2 * away, f + 3 * away),
    )
    slots = (0, jnp.where(mid, 1, 2), jnp.where(mid, 1, 3), jnp.where(mid, 2, 3))

    def copy_to(q, who, hop):
        if hop < OWN:
            to, there = {"dp": chips[hop]}, (q, who ^ hop)
        else:
            to = {"fsdp": planes[hop - OWN]}
            there = (slots[hop - OWN] if q == 0 else 2, who)
        return pltpu.make_async_remote_copy(
            src_ref=table_ref.at[0, q, who], dst_ref=table_ref.at[(0, *there)],
            send_sem=go_sem.at[q, who, hop], recv_sem=come_sem.at[there],
            device_id=to, device_id_type=MESH,
        )

    def pass_on(q, who):
        always, inner = hops_of(q, who)
        for hop in always:
            copy_to(q, who, hop).start()
        for hop in inner:
            pl.when(mid)(copy_to(q, who, hop).start)
        pltpu.make_async_remote_copy(
            src_ref=table_ref.at[0, q, who], dst_ref=table_ref.at[1, q, who],
            send_sem=gone_sem.at[0], recv_sem=share_sem.at[q, who],
            device_id={"crop": partner}, device_id_type=MESH,
        ).start()

    def arrive(core, q, who):
        block = table_ref.at[core, q, who]
        sem = share_sem.at[q, who] if core else come_sem.at[q, who]
        pltpu.make_async_copy(block, block, sem).wait()

    def unpack(core, q, who):
        value = decode(table_ref[core, q, who], rows, 0)
        high = value.astype(jnp.bfloat16)
        place = (c, partner)[core]
        wide = slice(q % 2 * columns, (q % 2 + 1) * columns)
        weight_ref[q // 2, who, 0, place, 0:size, wide] = high
        weight_ref[q // 2, who, 1, place, 0:size, wide] = (value - high.astype(jnp.float32)).astype(jnp.bfloat16)

    started = set()

    def multiply(group, chips_of):
        first, last = chips_of[0], chips_of[-1] + 1
        pair, wide = group[0] // 2, slice(group[0] % 2 * columns, (group[-1] % 2 + 1) * columns)
        right = weight_ref[pair, first:last, :, :, :, wide]
        right = right.reshape((last - first) * depth, right.shape[-1])
        fresh_sum = [q not in started for q in group]
        for k in range(C):
            left = left_ref[k, :, first * depth : last * depth]
            now = jnp.dot(left, right, preferred_element_type=jnp.float32)
            for number, q in enumerate(group):
                part = slice(q % 2 * columns, (q % 2 + 1) * columns)
                piece = now[:, number * columns : (number + 1) * columns]
                x_ref[pair, k, :, part] = piece if fresh_sum[number] else x_ref[pair, k, :, part] + piece
        started.update(group)

    pass_on(0, 0)
    for number in range(5):
        state_ref[number] = fresh[number]
    pixel_copy.wait()
    prepare(1, other_ref)
    seen = set()

    def finish(q, who):
        arrive(1, q, who)
        unpack(1, q, who)
        seen.add((q, who))
        for group, chips_of in GROUPS:
            if q in group and who in chips_of and all((p, w) in seen for p in group for w in chips_of):
                multiply(group, chips_of)

    unpack(0, 0, 0)
    ready = [(0, 0)]
    for q, who in ORDER:
        arrive(0, q, who)
        pass_on(q, who)
        unpack(0, q, who)
        ready.append((q, who))
        if len(ready) > LAG:
            finish(*ready.pop(0))
    for q, who in ready:
        finish(q, who)
    last = rows - (rows * DP * C - base)
    begin = last // 16 * 16
    for q in range(F):
        wide = slice(q % 2 * columns, (q % 2 + 1) * columns)
        for who in range(DP):
            @pl.when(chips[who] == DP - 1)
            def _():
                extra_ref[q] = (
                    weight_ref[q // 2, who, 0, C - 1, begin:size, wide].astype(jnp.float32)
                    + weight_ref[q // 2, who, 1, C - 1, begin:size, wide].astype(jnp.float32)
                )
    pltpu.make_async_copy(table_ref.at[0], table_ref.at[0], gone_sem.at[0]).wait()
    for copy in blocks + sends:
        copy.wait_send()
    for q, who in ((0, 0),) + ORDER:
        always, inner = hops_of(q, who)
        for hop in always:
            copy_to(q, who, hop).wait_send()
        for hop in inner:
            pl.when(mid)(copy_to(q, who, hop).wait_send)


def tokens_kernel(
    sizes, state_ref, x_ref, extra_ref, same_ref,
    student_out, moment1_out, moment2_out, teacher_out, update_out, tokens_ref,
    stage_ref, sems, state_sems,
):
    DP, F, C = sizes
    f = lax.axis_index("fsdp")
    rows = state_ref.shape[1]
    patch_count = x_ref.shape[2]
    copies = []
    for number, target in enumerate((student_out, moment1_out, moment2_out, teacher_out, update_out)):
        copy = pltpu.make_async_copy(state_ref.at[number], target, state_sems.at[number])
        copy.start()
        copies.append(copy)
    mid = (f == 1) | (f == 2)
    away = jnp.where(f < 2, 1, -1)

    def place(i):
        inner = jnp.where(i == f, 0, jnp.where(i == f + away, 1, jnp.where(i == f - away, 2, 3)))
        return jnp.where(mid, inner, jnp.abs(i - f))

    places = [place(i) for i in range(F)]
    offset = (rows - 4) % 16

    def extra(n):
        return jnp.concatenate([extra_ref[at, offset + n : offset + n + 1] for at in places], axis=1)

    gain, shift = extra(2), extra(3)

    def normed(x):
        average = jnp.mean(x, axis=-1, keepdims=True)
        centered = x - average
        variance = jnp.mean(centered * centered, axis=-1, keepdims=True)
        return centered * lax.rsqrt(variance + norm_epsilon) * gain + shift

    columns = extra_ref.shape[2]

    def block_of(at, source, start):
        lane = pl.multiple_of(lax.rem(at, 2) * columns, 128)
        return x_ref[at // 2, source, start : start + step, pl.ds(lane, columns)]

    class_row = normed(extra(0))
    for k in range(C):
        stage_ref[0:1, k] = class_row
    step = 32
    begun = 0
    for number, start in enumerate(range(0, patch_count, step)):
        for k in range(C):
            source = same_ref[0, k]
            x = jnp.concatenate([block_of(at, source, start) for at in places], axis=1)
            stage_ref[start + 1 : start + 1 + step, k] = normed(x)
        end = start + 1 + step
        copy = pltpu.make_async_copy(
            stage_ref.at[begun:end], tokens_ref.at[begun:end], sems.at[number]
        )
        copy.start()
        copies.append(copy)
        begun = end
    for copy in copies:
        copy.wait()


def kernels(grad_parts, student, teacher, moment1, moment2, step_count, pixels, assign, sizes):
    DP, F, C = sizes
    rows, columns = student.shape
    spare = padded_rows(rows)
    slot = lanes_of(spare)
    own = pixels[0, 0].T
    pix_size, patch_count = own.shape
    here = pl.BlockSpec(memory_space=pltpu.VMEM)
    anywhere = pl.BlockSpec(memory_space=pl.ANY)
    scalars = pl.BlockSpec(memory_space=pltpu.SMEM)
    count = DP * C
    slab = spare - (rows - 4) // 16 * 16
    inputs = [
        pltpu.with_memory_space_constraint(value, pltpu.HBM)
        for value in (grad_parts, own, student, teacher, moment1, moment2, assign)
    ]
    shared = pl.pallas_call(
        functools.partial(refresh_kernel, sizes),
        out_shape=(
            pltpu.VMEM((5, rows, columns), jnp.float32),
            pltpu.VMEM((F // 2, C, patch_count, 2 * columns), jnp.float32),
            pltpu.VMEM((F, slab, columns), jnp.float32),
            pltpu.SMEM((1, C), jnp.int32),
        ),
        in_specs=[anywhere] * 7 + [scalars],
        out_specs=(here,) * 3 + (scalars,),
        scratch_shapes=[
            pltpu.VMEM((C, F, DP, spare, columns), jnp.int16),
            pltpu.VMEM((F // 2, DP, 2, C, slot, 2 * columns), jnp.bfloat16),
            pltpu.VMEM((C, patch_count, count * 2 * slot), jnp.bfloat16),
            pltpu.VMEM((rows * (count - 1) + slot, patch_count), jnp.float32),
            pltpu.VMEM(own.shape, own.dtype),
            pltpu.VMEM(own.shape, own.dtype),
            pltpu.VMEM((DP, spare, columns), jnp.float32),
            pltpu.VMEM((DP, spare, columns), jnp.float32),
            pltpu.VMEM((DP, spare, columns), jnp.int16),
            pltpu.VMEM((DP, spare, columns), jnp.int16),
            pltpu.VMEM((spare, columns), jnp.float32),
            pltpu.VMEM((4, rows, columns), jnp.float32),
            pltpu.SMEM((1, C), jnp.int32),
            pltpu.SemaphoreType.DMA((6,)),
            pltpu.SemaphoreType.DMA((DP,)),
            pltpu.SemaphoreType.DMA((2, DP)),
            pltpu.SemaphoreType.DMA((DP,)),
            pltpu.SemaphoreType.DMA((DP,)),
            pltpu.SemaphoreType.DMA((2,)),
            pltpu.SemaphoreType.DMA((F, DP, OWN + F)),
            pltpu.SemaphoreType.DMA((F, DP)),
            pltpu.SemaphoreType.DMA((F, DP)),
            pltpu.SemaphoreType.DMA((1,)),
        ],
        compiler_params=pltpu.CompilerParams(
            collective_id=0, has_side_effects=True, vmem_limit_bytes=40 * 1024 * 1024
        ),
    )(*inputs, step_count)
    *results, tokens = pl.pallas_call(
        functools.partial(tokens_kernel, sizes),
        out_shape=(jax.ShapeDtypeStruct((rows, columns), jnp.float32),) * 5
        + (jax.ShapeDtypeStruct((patch_count + 1, C, columns * F), jnp.float32),),
        in_specs=[here] * 3 + [scalars],
        out_specs=(anywhere,) * 6,
        scratch_shapes=[
            pltpu.VMEM((patch_count + 1, C, columns * F), jnp.float32),
            pltpu.SemaphoreType.DMA((patch_count // 32,)),
            pltpu.SemaphoreType.DMA((5,)),
        ],
        compiler_params=pltpu.CompilerParams(vmem_limit_bytes=40 * 1024 * 1024),
    )(*(pltpu.with_memory_space_constraint(value, pltpu.VMEM) for value in shared[:3]), shared[3])
    return (*results, tokens.transpose(1, 0, 2)[None])


def shards(grad_parts, student, teacher, moment1, moment2, step_count, pixels, assign):
    gradient = lax.psum_scatter(grad_parts[0], ("dp", "crop"), scatter_dimension=0, tiled=True)
    student_new, first_moment, second_moment, teacher_new, update = optimize(
        gradient, student, teacher, moment1, moment2, step_count
    )
    column_block = lax.all_gather(teacher_new, "fsdp", axis=1, tiled=True)
    gathered = lax.all_gather(column_block, ("dp", "crop"), axis=0, tiled=True)
    own_tokens = embed(pixels[:, 0], gathered)
    both = lax.all_gather(own_tokens[:, None], "crop", axis=1, tiled=True)
    teacher_tokens = jnp.where((assign == 0)[:, :, None, None], both[:, 0:1], both[:, 1:2])
    return (student_new, first_moment, second_moment, teacher_new, update, teacher_tokens)


def solution(mesh):
    placed = (
        P(("dp", "crop"), None, "fsdp"),
        P(("dp", "crop"), "fsdp"),
        P(("dp", "crop"), "fsdp"),
        P(("dp", "crop"), "fsdp"),
        P(("dp", "crop"), "fsdp"),
        P(),
        P(("dp", "fsdp"), "crop", None, None),
        P(("dp", "fsdp"), None),
    )
    sizes = (mesh.shape["dp"], mesh.shape["fsdp"], mesh.shape["crop"])

    def run(*args):
        grad_parts, student, pixels = args[0], args[1], args[6]
        fits = (
            student.shape[1] % 128 == 0
            and padded_rows(student.shape[0]) <= student.shape[1]
            and pixels.shape[:2] == (1, 1)
            and grad_parts.shape[0] == 1
            and sizes[0] == 4
            and sizes[1] == 4
            and pixels.shape[2] % 32 == 0
            and windows_fit(student.shape[0], sizes[0] * sizes[2])
            and sizes[2] == 2
        )
        return kernels(*args, sizes) if fits else shards(*args)

    return jax.shard_map(
        run,
        mesh=mesh,
        in_specs=placed,
        out_specs=(
            P(("dp", "crop"), "fsdp"),
            P(("dp", "crop"), "fsdp"),
            P(("dp", "crop"), "fsdp"),
            P(("dp", "crop"), "fsdp"),
            P(("dp", "crop"), "fsdp"),
            P(("dp", "fsdp"), None, None, None),
        ),
        check_vma=False,
    )
```

```python
import functools
import math

import jax
import jax.numpy as jnp
from jax import lax
from jax.experimental import pallas as pl
from jax.experimental.pallas import tpu as pltpu
from jax.sharding import PartitionSpec as P

beta_one = 0.9
beta_two = 0.999
adam_epsilon = 1e-08
learn_rate = 0.001
weight_decay = 0.04
momentum_base = 0.992
plan_length = 625000.0
norm_epsilon = 1e-06


def optimize(gradient, student, teacher, moment1, moment2, step_count):
    step_value = step_count[0].astype(jnp.float32)
    first_moment = beta_one * moment1 + (1.0 - beta_one) * gradient
    second_moment = beta_two * moment2 + (1.0 - beta_two) * gradient * gradient
    first_fix = 1.0 - jnp.power(jnp.float32(beta_one), step_value)
    second_fix = 1.0 - jnp.power(jnp.float32(beta_two), step_value)
    update = (
        first_moment / first_fix / (jnp.sqrt(second_moment / second_fix) + adam_epsilon)
        + weight_decay * student
    )
    student_new = student - learn_rate * update
    momentum = (
        1.0 - (1.0 - momentum_base) * (jnp.cos(math.pi * step_value / plan_length) + 1.0) / 2.0
    )
    teacher_new = momentum * teacher + (1.0 - momentum) * student_new
    return (student_new, first_moment, second_moment, teacher_new, update)


def embed(patches, table):
    count = patches.shape[0]
    pix_size = patches.shape[2]
    patch_count = patches.shape[1]
    width = table.shape[1]
    weight = table[:pix_size]
    position = table[pix_size : pix_size + patch_count]
    extras = table[pix_size + patch_count :]
    flat_patches = patches.reshape(count * patch_count, pix_size).astype(jnp.float32)
    projected = jnp.dot(
        flat_patches, weight, precision=lax.Precision.HIGHEST, preferred_element_type=jnp.float32
    )
    projected = projected.reshape(count, patch_count, width) + extras[1] + position
    class_row = jnp.broadcast_to(extras[0], (count, 1, width))
    tokens = jnp.concatenate([class_row, projected], axis=1)
    average = jnp.mean(tokens, axis=-1, keepdims=True)
    centered = tokens - average
    variance = jnp.mean(centered * centered, axis=-1, keepdims=True)
    return centered * lax.rsqrt(variance + norm_epsilon) * extras[2] + extras[3]


LEVELS = 32767.0
CODES = 256.0
MESH = pl.DeviceIdType.MESH


def padded_rows(rows):
    return -(-(rows + 1) // 16) * 16


def lanes_of(count):
    return -(-count // 128) * 128


def windows_fit(rows, count):
    size = padded_rows(rows)
    return all(j * rows % 8 + rows <= size and j * rows // 8 * 8 + size <= rows * count for j in range(count))


def turned(count, width, offset):
    row = lax.broadcasted_iota(jnp.int32, (count, width), 0) - offset
    return jnp.where(row < 0, row + count, row)


def encode(value, rows, offset):
    count, width = value.shape
    row_index = turned(count, width, offset)
    value = jnp.where(row_index < rows, value, 0.0)
    top = jnp.maximum(jnp.max(jnp.abs(value), axis=1, keepdims=True), 1e-30)
    code = jnp.ceil(jnp.log2(top) * CODES + 0.01)
    scaled = value * (jnp.exp2(code * (-1.0 / CODES)) * LEVELS)
    lanes = lanes_of(count)
    lane = lax.broadcasted_iota(jnp.int32, (count, lanes), 1)
    near = jnp.where(row_index[:, :lanes] == lane, code, 0.0)
    code_row = jnp.sum(near, axis=0, keepdims=True)
    if width > lanes:
        rest = jnp.zeros((1, width - lanes), jnp.float32)
        code_row = jnp.concatenate([code_row, rest], axis=1)
    out = jnp.where(row_index == rows, jnp.broadcast_to(code_row, (count, width)), scaled)
    out = jnp.clip(jnp.round(out), -LEVELS, LEVELS)
    return out.astype(jnp.int32).astype(jnp.int16)


def decode(block, rows, offset):
    count, width = block.shape
    value = block.astype(jnp.int32).astype(jnp.float32)
    lanes = lanes_of(count)
    lane = lax.broadcasted_iota(jnp.int32, (count, lanes), 1)
    row_index = turned(count, lanes, offset)
    if isinstance(offset, int):
        code_row = value[rows : rows + 1, :lanes]
    else:
        code_row = jnp.sum(jnp.where(row_index == rows, value[:, :lanes], 0.0), axis=0, keepdims=True)
    near = jnp.where(row_index == lane, code_row, 0.0)
    code = jnp.sum(near, axis=1, keepdims=True)
    return value * (jnp.exp2(code * (1.0 / CODES)) * (1.0 / LEVELS))


OWN = 4
ORDER = (
    (1, 0), (0, 1), (0, 2), (2, 0), (3, 0), (0, 3), (1, 1), (1, 3), (1, 2), (2, 1), (2, 2),
    (3, 1), (3, 2), (2, 3), (3, 3),
)
GROUPS = (
    ((0, 1), (0,)), ((0, 1), (1, 2)), ((0, 1), (3,)), ((2, 3), (0,)), ((2, 3), (1, 2)), ((2, 3), (3,)),
)
LAG = 2
ARRIVE = (1, 2, 0)


def schedule(step_ref):
    step_value = jnp.full((8, 128), step_ref[0], jnp.int32).astype(jnp.float32)
    first_fix = 1.0 - jnp.power(jnp.full((8, 128), beta_one, jnp.float32), step_value)
    second_fix = 1.0 - jnp.power(jnp.full((8, 128), beta_two, jnp.float32), step_value)
    momentum = (
        1.0 - (1.0 - momentum_base) * (jnp.cos(math.pi * step_value / plan_length) + 1.0) / 2.0
    )
    return first_fix[0:1, 0:1], second_fix[0:1, 0:1], momentum[0:1, 0:1]


def step_of(gradient, student, teacher, moment1, moment2, step_ref):
    first_fix, second_fix, momentum = schedule(step_ref)
    first_moment = beta_one * moment1 + (1.0 - beta_one) * gradient
    second_moment = beta_two * moment2 + (1.0 - beta_two) * gradient * gradient
    update = (
        first_moment / first_fix / (jnp.sqrt(second_moment / second_fix) + adam_epsilon)
        + weight_decay * student
    )
    student_new = student - learn_rate * update
    teacher_new = momentum * teacher + (1.0 - momentum) * student_new
    return student_new, first_moment, second_moment, teacher_new, update


def hops_of(q, who):
    if who == 0:
        along = (OWN + 1, OWN + 3, OWN + 2) if q == 0 else ()
        return along + ((3,) if q in (0, 3) else ()) + (1, 2), ()
    if who == 3 and q == 0:
        return (OWN + 1,), (OWN + 2,)
    if who == 3 and q == 1:
        return (), (OWN + 2,)
    return (), ()


def refresh_kernel(
    sizes, grad_ref, pixel_ref, student_ref, teacher_ref, moment1_ref, moment2_ref, pick_ref, step_ref,
    state_ref, x_ref, extra_ref, same_ref,
    table_ref, weight_ref, left_ref, pixels_ref, mine_ref, other_ref, half_ref, pre_ref, out_ref, in_ref,
    space_ref, held_ref, pick_now,
    load_sem, half_sem, pair_sem, out_sem, in_sem, pix_sem, go_sem, come_sem, share_sem, gone_sem,
):
    DP, F, C = sizes
    (rows, columns), size = student_ref.shape, table_ref.shape[3]
    d, f, c = lax.axis_index("dp"), lax.axis_index("fsdp"), lax.axis_index("crop")
    partner = lax.rem(c + 1, C)

    barrier = pltpu.get_barrier_semaphore()
    pl.semaphore_signal(barrier, inc=1, device_id={"crop": partner}, device_id_type=MESH)
    for r in range(1, DP):
        pl.semaphore_signal(barrier, inc=1, device_id={"dp": lax.rem(d + r, DP)}, device_id_type=MESH)
    for r in range(1, F):
        pl.semaphore_signal(barrier, inc=1, device_id={"fsdp": lax.rem(f + r, F)}, device_id_type=MESH)

    row, column = d // 2, lax.rem(d, 2)
    chips = (
        d,
        row * 2 + 1 - column,
        (1 - row) * 2 + column,
        (1 - row) * 2 + 1 - column,
    )
    order = (3, 1, 2, 0)

    def window(at, core):
        start = (at * C + core) * rows // 8 * 8
        return grad_ref.at[0, pl.ds(pl.multiple_of(start, 8), size)]

    halves = []
    for r in order:
        copy = pltpu.make_async_copy(window(chips[r], c), half_ref.at[r], half_sem.at[r])
        copy.start()
        halves.append(copy)
    loads = []
    for source, target in (
        (pick_ref, pick_now), (pixel_ref, mine_ref), (student_ref, held_ref.at[0]),
        (teacher_ref, held_ref.at[1]), (moment1_ref, held_ref.at[2]), (moment2_ref, held_ref.at[3]),
    ):
        copy = pltpu.make_async_copy(source, target, load_sem.at[len(loads)])
        copy.start()
        loads.append(copy)

    pl.semaphore_wait(barrier, DP - 1 + 1 + F - 1)
    sends = []
    for r in order:
        copy = pltpu.make_async_remote_copy(
            src_ref=window(chips[r], partner), dst_ref=pre_ref.at[r],
            send_sem=pair_sem.at[0, r], recv_sem=pair_sem.at[1, r],
            device_id={"crop": partner}, device_id_type=MESH,
        )
        copy.start()
        sends.append(copy)
    blocks = []
    total = None
    offset = (d * C + c) * rows % 8
    for number, r in enumerate(order):
        at = chips[r]
        halves[number].wait()
        sends[number].wait_recv()
        chip = half_ref[r] + pre_ref[r]
        if r == 0:
            total = chip
            break
        out_ref[r] = encode(chip, rows, (at * C + c) * rows % 8)
        copy = pltpu.make_async_remote_copy(
            src_ref=out_ref.at[r], dst_ref=in_ref.at[r],
            send_sem=out_sem.at[r], recv_sem=in_sem.at[r],
            device_id={"dp": at}, device_id_type=MESH,
        )
        copy.start()
        blocks.append(copy)
    pixel_copy = pltpu.make_async_remote_copy(
        src_ref=pixel_ref, dst_ref=other_ref, send_sem=pix_sem.at[0], recv_sem=pix_sem.at[1],
        device_id={"crop": partner}, device_id_type=MESH,
    )
    pixel_copy.start()
    for copy in loads:
        copy.wait()

    slot = weight_ref.shape[4]
    depth = 2 * C * slot
    pix_size, patch_count = pixel_ref.shape
    base = pix_size + patch_count

    def prepare(k, source_ref):
        pixels_ref[0:pix_size] = source_ref[...].astype(jnp.float32)
        pixels_ref[pix_size:] = jnp.zeros((pixels_ref.shape[0] - pix_size, patch_count), jnp.float32)
        for j in range(DP * C):
            lane = lax.broadcasted_iota(jnp.int32, (patch_count, slot), 1)
            patch = lax.broadcasted_iota(jnp.int32, (patch_count, slot), 0)
            at = lane + j * rows
            inside = lane < rows
            one = inside & ((at == base + 1) | ((at < base) & (at - pix_size == patch)))
            block = jnp.where(one, 1.0, 0.0)
            if j * rows < pix_size:
                block = block + jnp.where(inside, pixels_ref[j * rows : j * rows + slot].T, 0.0)
            near = lax.rem(j // C // 2 + row, 2) * 2 + lax.rem(j // C + column, 2)
            block = block.astype(jnp.bfloat16)
            for level in range(2):
                start = near * depth + (level * C + j % C) * slot
                left_ref[k, :, pl.ds(pl.multiple_of(start, 128), slot)] = block

    blank = jnp.zeros((F // 2, DP, 2, C, slot - size, weight_ref.shape[5]), jnp.bfloat16)
    weight_ref[:, :, :, :, size:] = blank
    prepare(0, mine_ref)
    for k in range(C):
        same_ref[0, k] = jnp.where(pick_now[0, k] == c, 0, 1)
    for number in ARRIVE:
        blocks[number].wait_recv()
        total = total + decode(in_ref[order[number]], rows, offset)
    gradient = pltpu.roll(total, lax.rem(size - offset, size), 0)[0:rows]
    fresh = step_of(gradient, held_ref[0], held_ref[1], held_ref[2], held_ref[3], step_ref)
    space_ref[rows:] = jnp.zeros((size - rows, space_ref.shape[1]), jnp.float32)
    space_ref[0:rows] = fresh[3]
    table_ref[0, 0, 0] = encode(space_ref[...], rows, 0)

    mid = (f == 1) | (f == 2)
    away = jnp.where(f < 2, 1, -1)
    planes = (
        f,
        f + away,
        jnp.where(mid, f - away, f + 2 * away),
        jnp.where(mid, f + 2 * away, f + 3 * away),
    )
    slots = (0, jnp.where(mid, 1, 2), jnp.where(mid, 1, 3), jnp.where(mid, 2, 3))

    def copy_to(q, who, hop):
        if hop < OWN:
            to, there = {"dp": chips[hop]}, (q, who ^ hop)
        else:
            to = {"fsdp": planes[hop - OWN]}
            there = (slots[hop - OWN] if q == 0 else 2, who)
        return pltpu.make_async_remote_copy(
            src_ref=table_ref.at[0, q, who], dst_ref=table_ref.at[(0, *there)],
            send_sem=go_sem.at[q, who, hop], recv_sem=come_sem.at[there],
            device_id=to, device_id_type=MESH,
        )

    def pass_on(q, who):
        always, inner = hops_of(q, who)
        for hop in always:
            copy_to(q, who, hop).start()
        for hop in inner:
            pl.when(mid)(copy_to(q, who, hop).start)
        pltpu.make_async_remote_copy(
            src_ref=table_ref.at[0, q, who], dst_ref=table_ref.at[1, q, who],
            send_sem=gone_sem.at[0], recv_sem=share_sem.at[q, who],
            device_id={"crop": partner}, device_id_type=MESH,
        ).start()

    def arrive(core, q, who):
        block = table_ref.at[core, q, who]
        sem = share_sem.at[q, who] if core else come_sem.at[q, who]
        pltpu.make_async_copy(block, block, sem).wait()

    def unpack(core, q, who):
        value = decode(table_ref[core, q, who], rows, 0)
        high = value.astype(jnp.bfloat16)
        place = (c, partner)[core]
        wide = slice(q % 2 * columns, (q % 2 + 1) * columns)
        weight_ref[q // 2, who, 0, place, 0:size, wide] = high
        weight_ref[q // 2, who, 1, place, 0:size, wide] = (value - high.astype(jnp.float32)).astype(jnp.bfloat16)

    started = set()

    def multiply(group, chips_of):
        first, last = chips_of[0], chips_of[-1] + 1
        pair, wide = group[0] // 2, slice(group[0] % 2 * columns, (group[-1] % 2 + 1) * columns)
        right = weight_ref[pair, first:last, :, :, :, wide]
        right = right.reshape((last - first) * depth, right.shape[-1])
        fresh_sum = [q not in started for q in group]
        for k in range(C):
            left = left_ref[k, :, first * depth : last * depth]
            now = jnp.dot(left, right, preferred_element_type=jnp.float32)
            for number, q in enumerate(group):
                part = slice(q % 2 * columns, (q % 2 + 1) * columns)
                piece = now[:, number * columns : (number + 1) * columns]
                x_ref[pair, k, :, part] = piece if fresh_sum[number] else x_ref[pair, k, :, part] + piece
        started.update(group)

    pass_on(0, 0)
    for number in range(5):
        state_ref[number] = fresh[number]
    pixel_copy.wait()
    prepare(1, other_ref)
    seen = set()

    def finish(q, who):
        arrive(1, q, who)
        unpack(1, q, who)
        seen.add((q, who))
        for group, chips_of in GROUPS:
            if q in group and who in chips_of and all((p, w) in seen for p in group for w in chips_of):
                multiply(group, chips_of)

    unpack(0, 0, 0)
    ready = [(0, 0)]
    for q, who in ORDER:
        arrive(0, q, who)
        pass_on(q, who)
        unpack(0, q, who)
        ready.append((q, who))
        if len(ready) > LAG:
            finish(*ready.pop(0))
    for q, who in ready:
        finish(q, who)
    last = rows - (rows * DP * C - base)
    begin = last // 16 * 16
    for q in range(F):
        wide = slice(q % 2 * columns, (q % 2 + 1) * columns)
        for who in range(DP):
            @pl.when(chips[who] == DP - 1)
            def _():
                extra_ref[q] = (
                    weight_ref[q // 2, who, 0, C - 1, begin:size, wide].astype(jnp.float32)
                    + weight_ref[q // 2, who, 1, C - 1, begin:size, wide].astype(jnp.float32)
                )
    pltpu.make_async_copy(table_ref.at[0], table_ref.at[0], gone_sem.at[0]).wait()
    for copy in blocks + sends:
        copy.wait_send()
    for q, who in ((0, 0),) + ORDER:
        always, inner = hops_of(q, who)
        for hop in always:
            copy_to(q, who, hop).wait_send()
        for hop in inner:
            pl.when(mid)(copy_to(q, who, hop).wait_send)


def tokens_kernel(
    sizes, state_ref, x_ref, extra_ref, same_ref,
    student_out, moment1_out, moment2_out, teacher_out, update_out, tokens_ref,
    stage_ref, sems, state_sems,
):
    DP, F, C = sizes
    f = lax.axis_index("fsdp")
    rows = state_ref.shape[1]
    patch_count = x_ref.shape[2]
    copies = []
    for number, target in enumerate((student_out, moment1_out, moment2_out, teacher_out, update_out)):
        copy = pltpu.make_async_copy(state_ref.at[number], target, state_sems.at[number])
        copy.start()
        copies.append(copy)
    mid = (f == 1) | (f == 2)
    away = jnp.where(f < 2, 1, -1)

    def place(i):
        inner = jnp.where(i == f, 0, jnp.where(i == f + away, 1, jnp.where(i == f - away, 2, 3)))
        return jnp.where(mid, inner, jnp.abs(i - f))

    places = [place(i) for i in range(F)]
    offset = (rows - 4) % 16

    def extra(n):
        return jnp.concatenate([extra_ref[at, offset + n : offset + n + 1] for at in places], axis=1)

    gain, shift = extra(2), extra(3)

    def normed(x):
        average = jnp.mean(x, axis=-1, keepdims=True)
        centered = x - average
        variance = jnp.mean(centered * centered, axis=-1, keepdims=True)
        return centered * lax.rsqrt(variance + norm_epsilon) * gain + shift

    columns = extra_ref.shape[2]

    def block_of(at, source, start):
        lane = pl.multiple_of(lax.rem(at, 2) * columns, 128)
        return x_ref[at // 2, source, start : start + step, pl.ds(lane, columns)]

    class_row = normed(extra(0))
    for k in range(C):
        stage_ref[0:1, k] = class_row
    step = 32
    begun = 0
    for number, start in enumerate(range(0, patch_count, step)):
        for k in range(C):
            source = same_ref[0, k]
            x = jnp.concatenate([block_of(at, source, start) for at in places], axis=1)
            stage_ref[start + 1 : start + 1 + step, k] = normed(x)
        end = start + 1 + step
        copy = pltpu.make_async_copy(
            stage_ref.at[begun:end], tokens_ref.at[begun:end], sems.at[number]
        )
        copy.start()
        copies.append(copy)
        begun = end
    for copy in copies:
        copy.wait()


def kernels(grad_parts, student, teacher, moment1, moment2, step_count, pixels, assign, sizes):
    DP, F, C = sizes
    rows, columns = student.shape
    spare = padded_rows(rows)
    slot = lanes_of(spare)
    own = pixels[0, 0].T
    pix_size, patch_count = own.shape
    here = pl.BlockSpec(memory_space=pltpu.VMEM)
    anywhere = pl.BlockSpec(memory_space=pl.ANY)
    scalars = pl.BlockSpec(memory_space=pltpu.SMEM)
    count = DP * C
    slab = spare - (rows - 4) // 16 * 16
    inputs = [
        pltpu.with_memory_space_constraint(value, pltpu.HBM)
        for value in (grad_parts, own, student, teacher, moment1, moment2, assign)
    ]
    shared = pl.pallas_call(
        functools.partial(refresh_kernel, sizes),
        out_shape=(
            pltpu.VMEM((5, rows, columns), jnp.float32),
            pltpu.VMEM((F // 2, C, patch_count, 2 * columns), jnp.float32),
            pltpu.VMEM((F, slab, columns), jnp.float32),
            pltpu.SMEM((1, C), jnp.int32),
        ),
        in_specs=[anywhere] * 7 + [scalars],
        out_specs=(here,) * 3 + (scalars,),
        scratch_shapes=[
            pltpu.VMEM((C, F, DP, spare, columns), jnp.int16),
            pltpu.VMEM((F // 2, DP, 2, C, slot, 2 * columns), jnp.bfloat16),
            pltpu.VMEM((C, patch_count, count * 2 * slot), jnp.bfloat16),
            pltpu.VMEM((rows * (count - 1) + slot, patch_count), jnp.float32),
            pltpu.VMEM(own.shape, own.dtype),
            pltpu.VMEM(own.shape, own.dtype),
            pltpu.VMEM((DP, spare, columns), jnp.float32),
            pltpu.VMEM((DP, spare, columns), jnp.float32),
            pltpu.VMEM((DP, spare, columns), jnp.int16),
            pltpu.VMEM((DP, spare, columns), jnp.int16),
            pltpu.VMEM((spare, columns), jnp.float32),
            pltpu.VMEM((4, rows, columns), jnp.float32),
            pltpu.SMEM((1, C), jnp.int32),
            pltpu.SemaphoreType.DMA((6,)),
            pltpu.SemaphoreType.DMA((DP,)),
            pltpu.SemaphoreType.DMA((2, DP)),
            pltpu.SemaphoreType.DMA((DP,)),
            pltpu.SemaphoreType.DMA((DP,)),
            pltpu.SemaphoreType.DMA((2,)),
            pltpu.SemaphoreType.DMA((F, DP, OWN + F)),
            pltpu.SemaphoreType.DMA((F, DP)),
            pltpu.SemaphoreType.DMA((F, DP)),
            pltpu.SemaphoreType.DMA((1,)),
        ],
        compiler_params=pltpu.CompilerParams(
            collective_id=0, has_side_effects=True, vmem_limit_bytes=40 * 1024 * 1024
        ),
    )(*inputs, step_count)
    *results, tokens = pl.pallas_call(
        functools.partial(tokens_kernel, sizes),
        out_shape=(jax.ShapeDtypeStruct((rows, columns), jnp.float32),) * 5
        + (jax.ShapeDtypeStruct((patch_count + 1, C, columns * F), jnp.float32),),
        in_specs=[here] * 3 + [scalars],
        out_specs=(anywhere,) * 6,
        scratch_shapes=[
            pltpu.VMEM((patch_count + 1, C, columns * F), jnp.float32),
            pltpu.SemaphoreType.DMA((patch_count // 32,)),
            pltpu.SemaphoreType.DMA((5,)),
        ],
        compiler_params=pltpu.CompilerParams(vmem_limit_bytes=40 * 1024 * 1024),
    )(*(pltpu.with_memory_space_constraint(value, pltpu.VMEM) for value in shared[:3]), shared[3])
    return (*results, tokens.transpose(1, 0, 2)[None])


def shards(grad_parts, student, teacher, moment1, moment2, step_count, pixels, assign):
    gradient = lax.psum_scatter(grad_parts[0], ("dp", "crop"), scatter_dimension=0, tiled=True)
    student_new, first_moment, second_moment, teacher_new, update = optimize(
        gradient, student, teacher, moment1, moment2, step_count
    )
    column_block = lax.all_gather(teacher_new, "fsdp", axis=1, tiled=True)
    gathered = lax.all_gather(column_block, ("dp", "crop"), axis=0, tiled=True)
    own_tokens = embed(pixels[:, 0], gathered)
    both = lax.all_gather(own_tokens[:, None], "crop", axis=1, tiled=True)
    teacher_tokens = jnp.where((assign == 0)[:, :, None, None], both[:, 0:1], both[:, 1:2])
    return (student_new, first_moment, second_moment, teacher_new, update, teacher_tokens)


def solution(mesh):
    placed = (
        P(("dp", "crop"), None, "fsdp"),
        P(("dp", "crop"), "fsdp"),
        P(("dp", "crop"), "fsdp"),
        P(("dp", "crop"), "fsdp"),
        P(("dp", "crop"), "fsdp"),
        P(),
        P(("dp", "fsdp"), "crop", None, None),
        P(("dp", "fsdp"), None),
    )
    sizes = (mesh.shape["dp"], mesh.shape["fsdp"], mesh.shape["crop"])

    def run(*args):
        grad_parts, student, pixels = args[0], args[1], args[6]
        fits = (
            student.shape[1] % 128 == 0
            and padded_rows(student.shape[0]) <= student.shape[1]
            and pixels.shape[:2] == (1, 1)
            and grad_parts.shape[0] == 1
            and sizes[0] == 4
            and sizes[1] == 4
            and pixels.shape[2] % 32 == 0
            and windows_fit(student.shape[0], sizes[0] * sizes[2])
            and sizes[2] == 2
        )
        return kernels(*args, sizes) if fits else shards(*args)

    return jax.shard_map(
        run,
        mesh=mesh,
        in_specs=placed,
        out_specs=(
            P(("dp", "crop"), "fsdp"),
            P(("dp", "crop"), "fsdp"),
            P(("dp", "crop"), "fsdp"),
            P(("dp", "crop"), "fsdp"),
            P(("dp", "crop"), "fsdp"),
            P(("dp", "fsdp"), None, None, None),
        ),
        check_vma=False,
    )
```
